32 devices in a mesh: lat: 4 (over y, core), lon: 8 (over z, x).
Axes of the slice: x: 2, y: 2, z: 4, core: 2. Of those that a mesh axis runs over, the one named last changes fastest.
Arguments:
- control: bfloat16 [80, 32, 64, 512], P(None, None, 'lon', 'lat'), may hold values from -6 to 6
- ensemble: bfloat16 [80, 32, 64, 512], P(None, None, 'lon', 'lat'), may hold values from -1.1953125 to 1.1953125
- level_mix: bfloat16 [32, 32], replicated, may hold values from -1 to 1
- lat_taps: float32 [4], replicated, may hold values from 0.1 to 0.6
- lon_taps: float32 [4], replicated, may hold values from 0.1 to 0.6
- obs_location: int32 [8, 4, 2048], P('lon', 'lat'), may hold values from 0 to 32767
- obs_count: int32 [8, 4], P('lon', 'lat'), may hold values from 512 to 2048, as said below
- obs_keep: int32 [8, 4, 2048], P('lon', 'lat'), may hold values 0 or 1
- innovation: float32 [8, 4, 2048], P('lon', 'lat'), may hold values from -6 to 6
- obs_weight: float32 [8, 4, 2048], P('lon', 'lat'), may hold values from 0.25 to 4
Outputs:
- gradient: float32 [80, 32, 64, 512], P(None, None, 'lon', 'lat')
- upper_factor: float32 [80, 80], replicated
The draws below stay inside these ranges and needn't reach their ends.
Inputs may be any that keep to these rules, and one draw needn't show every extreme that they name: `obs_count`: live slots of a tile come first; some tile has all 2048 slots live.
All inputs are finite; a program needn't handle non-finite values. No bound on the sum of `obs_keep` on one device may be relied on, other than what follows from the above.
Results may differ from the reference program's by a relative error of at most 0.0028.
Values may be sent and summed in bfloat16 or wider, within the bound.
A program may use at most 128 MiB of HBM per device.

```python
import math
import jax
import jax.numpy as jnp
from jax import lax

MEMBERS = 80
LEVELS = 32
LON_DEV = 8
LAT_DEV = 128
OBS_DEV = 2048
TILES_LON = 8
TILES_LAT = 4
NLON = 64
NLAT = 512
OBS_ALL = 65536


def draw_obs_count(key, part):
    lon_index = jnp.arange(TILES_LON, dtype=jnp.int32)[:, None]
    lat_index = jnp.arange(TILES_LAT, dtype=jnp.int32)[None, :]
    span_all = max(TILES_LON + TILES_LAT - 2, 1)
    quarter = OBS_DEV // 4
    rising = (OBS_DEV - quarter) * (lon_index + lat_index) // span_all
    jitter = jax.random.randint(key, (TILES_LON, TILES_LAT), 0, OBS_DEV // 8 + 1, dtype=jnp.int32)
    return jnp.minimum(quarter + rising + jitter, OBS_DEV).astype(jnp.int32)


def touch_ends(entries, key, least, high):
    shape = entries.shape
    spot = [jax.random.randint(jax.random.fold_in(key, axis), (), 0, shape[axis]) for axis in range(len(shape))]
    entries = entries.at[tuple(spot)].set(least)
    longest = shape.index(max(shape))
    spot[longest] = (spot[longest] + 1) % shape[longest]
    return entries.at[tuple(spot)].set(high)


def levels(own_key, shape, pieces, least, high):
    factor_of, own = 1.0, jax.random.fold_in(own_key, 6)
    for dim, parts in pieces:
        steps = jnp.exp(jax.random.uniform(jax.random.fold_in(own, dim), (parts,), jnp.float32, least / len(pieces), high / len(pieces)))
        factor_of = factor_of * jnp.repeat(steps, shape[dim] // parts).reshape([-1 if axis == dim else 1 for axis in range(len(shape))])
    return factor_of


def centred(key, shape, scale, bound, pieces=(), kind=jnp.bfloat16):
    drawn = jax.random.normal(key, shape, jnp.float32) * scale
    if len(pieces) > 0:
        drawn = levels(key, shape, pieces, -0.22, 0.18) * drawn
    return jnp.clip(drawn, min=-bound, max=bound).astype(kind)


def setup_inputs(seed: int = 0) -> dict:
    key_list = jax.random.split(jax.random.key(seed), 11)
    control = centred(key_list[0], (MEMBERS, LEVELS, NLON, NLAT), 1.0, 6.0, ((2, 8), (3, 4)))
    ensemble = centred(key_list[1], (MEMBERS, LEVELS, NLON, NLAT), 0.2, 1.1953125, ((2, 8), (3, 4)))
    level_mix = centred(key_list[2], (LEVELS, LEVELS), LEVELS ** -0.5, 1.0)
    lat_taps = jnp.clip(jnp.exp(jax.random.uniform(key_list[3], (4,), jnp.float32, math.log(0.1), math.log(0.6))), 0.1, 0.6)
    lon_taps = jnp.clip(jnp.exp(jax.random.uniform(key_list[4], (4,), jnp.float32, math.log(0.1), math.log(0.6))), 0.1, 0.6)
    obs_location = touch_ends(jax.random.randint(key_list[5], (TILES_LON, TILES_LAT, OBS_DEV), 0, LEVELS * LON_DEV * LAT_DEV), jax.random.fold_in(key_list[5], 1), 0, (LEVELS * LON_DEV * LAT_DEV) - 1).astype(jnp.int32)
    obs_count = draw_obs_count(jax.random.fold_in(key_list[10], 71), 0)
    obs_keep = touch_ends((jax.random.randint(key_list[7], (TILES_LON, TILES_LAT, OBS_DEV), 0, 8) < 7).astype(jnp.int32), jax.random.fold_in(key_list[7], 1), 0, 1)
    innovation = centred(key_list[8], (TILES_LON, TILES_LAT, OBS_DEV), 1.0, 6.0, ((0, 8), (1, 4)), jnp.float32)
    obs_weight = jnp.clip(jnp.exp(math.log(4.0) - 2.7725887 * jax.random.uniform(key_list[9], (TILES_LON, TILES_LAT, OBS_DEV), jnp.float32) ** levels(key_list[9], (TILES_LON, TILES_LAT, OBS_DEV), ((0, 8), (1, 4)), -0.2, 0.2)), 0.25, 4.0)
    return {"control": control, "ensemble": ensemble, "level_mix": level_mix, "lat_taps": lat_taps, "lon_taps": lon_taps, "obs_location": obs_location, "obs_count": obs_count, "obs_keep": obs_keep, "innovation": innovation, "obs_weight": obs_weight}


OFFSETS = (-2, -1, 1, 2)

def shifted_sum(field, weights, dimension, direction, periodic):
    extent = field.shape[dimension]
    summed = field
    widths = [(0, 0)] * field.ndim
    widths[dimension] = (2, 2)
    padded = jnp.pad(field, widths)
    for position in range(4):
        shift = direction * OFFSETS[position]
        if periodic:
            moved = jnp.roll(field, -shift, axis=dimension)
        else:
            moved = lax.slice_in_dim(padded, 2 + shift, 2 + shift + extent, axis=dimension)
        summed = summed + weights[position] * moved
    return summed

def reference(control, ensemble, level_mix, lat_taps, lon_taps, obs_location, obs_count, obs_keep, innovation, obs_weight):

    def forward_member(carried, paired):
        control_m, ensemble_m = paired
        mixed_m = jnp.dot(level_mix.astype(jnp.float32), control_m.reshape(LEVELS, -1).astype(jnp.float32), preferred_element_type=jnp.float32).astype(jnp.bfloat16)
        mixed_f = lax.optimization_barrier(mixed_m).astype(jnp.float32).reshape(LEVELS, NLON, NLAT)
        rowpass = shifted_sum(mixed_f, lat_taps, 2, 1, False)
        localized = shifted_sum(rowpass, lon_taps, 1, 1, True)
        return (carried + ensemble_m.astype(jnp.float32) * localized, None)
    increment, unused = lax.scan(forward_member, jnp.zeros((LEVELS, NLON, NLAT), jnp.float32), (control, ensemble))
    tile_lon = jnp.arange(TILES_LON, dtype=jnp.int32)[:, None, None]
    tile_lat = jnp.arange(TILES_LAT, dtype=jnp.int32)[None, :, None]
    level_of = obs_location // (LON_DEV * LAT_DEV)
    column_of = tile_lon * LON_DEV + obs_location // LAT_DEV % LON_DEV
    row_of = tile_lat * LAT_DEV + obs_location % LAT_DEV
    flat_index = ((level_of * NLON + column_of) * NLAT + row_of).astype(jnp.int32).reshape(-1)
    slot_ids = jnp.arange(OBS_DEV, dtype=jnp.int32)[None, None, :]
    live_slots = (slot_ids < obs_count[:, :, None]).astype(jnp.float32) * obs_keep.astype(jnp.float32)
    weights = (live_slots * obs_weight).reshape(-1)
    misfit = weights * (increment.reshape(-1)[flat_index] - innovation.reshape(-1))
    pulled = jnp.zeros((LEVELS * NLON * NLAT,), jnp.float32).at[flat_index].add(misfit).reshape(LEVELS, NLON, NLAT)

    def adjoint_member(paired):
        control_m, ensemble_m = paired
        pulled_m = (ensemble_m.astype(jnp.float32) * pulled).astype(jnp.bfloat16)
        pulled_f = lax.optimization_barrier(pulled_m).astype(jnp.float32)
        colpass = shifted_sum(pulled_f, lon_taps, 1, -1, True)
        spread = shifted_sum(colpass, lat_taps, 2, -1, False).astype(jnp.bfloat16)
        mixed_back = jnp.dot(level_mix.T.astype(jnp.float32), spread.reshape(LEVELS, -1).astype(jnp.float32), preferred_element_type=jnp.float32)
        return control_m.astype(jnp.float32) + mixed_back.reshape(LEVELS, NLON, NLAT)
    gradient = lax.map(adjoint_member, (control, ensemble))
    columns = ensemble.reshape(MEMBERS, -1)[:, flat_index]
    anomaly = columns.astype(jnp.float32) * jnp.sqrt(weights)[None, :]
    gram = jnp.dot(anomaly, anomaly.T, precision=lax.Precision.HIGHEST)
    identity = jnp.eye(MEMBERS, dtype=jnp.float32)
    system = identity + MEMBERS / OBS_ALL * gram
    upper_factor = jnp.linalg.cholesky(system).T
    return (gradient, upper_factor)
```

```python
import functools

import jax
import jax.numpy as jnp
from jax import lax
from jax.experimental import pallas as pl
from jax.experimental.pallas import tpu as pltpu
from jax.sharding import PartitionSpec as P

OFFSETS = (-2, -1, 1, 2)
F32, BF = jnp.float32, jnp.bfloat16
MIB = 1024 * 1024
MESH = pl.DeviceIdType.MESH


def nn(a, b):
    return jnp.dot(a, b, preferred_element_type=F32)


def nt(a, b):
    return lax.dot_general(a, b, (((1,), (1,)), ((), ())), preferred_element_type=F32)


def tn(a, b):
    return lax.dot_general(a, b, (((0,), (0,)), ((), ())), preferred_element_type=F32)


def split(x):
    hi = x.astype(BF)
    return hi, (x - hi.astype(F32)).astype(BF)


def iota(shape, axis):
    return lax.broadcasted_iota(jnp.int32, shape, axis)


def band(diff, taps_ref, base, sign):
    out = jnp.where(diff == 0, 1.0, 0.0)
    for t, offset in enumerate(OFFSETS):
        out = out + jnp.where(diff == sign * offset, taps_ref[base + t], 0.0)
    return out


def halo_place(h, levels, cols):
    side = h // (2 * levels)
    rest = h - side * 2 * levels
    d = rest // levels
    return rest - d * levels, d + side * (cols - 2), d - 2 + side * (cols + 2)


def setup_kernel(dims, taps_ref, count_ref, mix_ref, place_ref, keep_ref, weight_ref, innov_ref,
                 kf_ref, ka_ref, lf_ref, la_ref, q_ref, v_ref, meta_ref, start_ref):
    levels, cols, lanes = dims
    rows, half = levels * cols, 2 * levels
    ext = rows + 2 * half

    def ext_level_col(x):
        k, own, outer = halo_place(x - rows, levels, cols)
        inside = x < rows
        xk = x // cols
        return jnp.where(inside, xk, k), jnp.where(inside, x - xk * cols, own), jnp.where(
            inside, x - xk * cols, outer)

    mix = mix_ref[...]
    level, _, col = ext_level_col(iota((ext, rows), 0))
    y = iota((ext, rows), 1)
    taps = band((y - y // cols * cols) - col, taps_ref, 4, 1)
    pick = (ext_level_col(iota((ext, levels), 0))[0] == iota((ext, levels), 1)).astype(F32).astype(BF)
    put = (iota((levels, rows), 1) // cols == iota((levels, rows), 0)).astype(F32).astype(BF)
    hi, lo = split(nn(nn(pick, mix).astype(BF), put) * taps)
    kf_ref[0] = hi
    kf_ref[1] = lo
    level, _, col = ext_level_col(iota((rows, ext), 1))
    y = iota((rows, ext), 0)
    taps = band((y - y // cols * cols) - col, taps_ref, 4, 1)
    pick = (ext_level_col(iota((levels, ext), 1))[0] == iota((levels, ext), 0)).astype(F32).astype(BF)
    put = (iota((rows, levels), 0) // cols == iota((rows, levels), 1)).astype(F32).astype(BF)
    hi, lo = split(nn(put, nn(mix.T, pick).astype(BF)) * taps)
    ka_ref[0] = hi
    ka_ref[1] = lo
    diff = iota((lanes, lanes), 0) - iota((lanes, lanes), 1)
    lf_ref[...] = jnp.concatenate(split(band(diff, taps_ref, 0, 1)), axis=0)
    la_ref[...] = jnp.concatenate(split(band(diff, taps_ref, 0, -1)), axis=0)

    slots = place_ref.shape[1]
    chunk = 512 if slots % 512 == 0 else slots
    ids = iota((ext, chunk), 0)
    ids_level, ids_col, _ = ext_level_col(iota((ext, 1), 0))
    ids = jnp.broadcast_to(ids_level * cols + ids_col, (ext, chunk))
    lane_ids = iota((lanes, chunk), 0)
    total = jnp.zeros((ext, 4 * lanes), F32)
    for s in range(0, slots, chunk):
        place = place_ref[:, s : s + chunk]
        r = place // lanes
        c = place - r * lanes
        live = (iota((1, chunk), 1) + s < count_ref[0, 0]).astype(F32) * keep_ref[:, s : s + chunk].astype(F32)
        q = live * weight_ref[:, s : s + chunk]
        v = q * innov_ref[:, s : s + chunk]
        hit = lane_ids == c
        parts = []
        for x in (q, v):
            for part in split(x):
                parts.append(jnp.where(hit, part.astype(F32), 0.0).astype(BF))
        total = total + nt((ids == r).astype(F32).astype(BF), jnp.concatenate(parts, axis=0))
    q = total[:, :lanes] + total[:, lanes : 2 * lanes]
    v = total[:, 2 * lanes : 3 * lanes] + total[:, 3 * lanes :]
    q_ref[...] = q[:rows]
    v_ref[...] = v[:rows]
    held = q[rows:] > 0.0
    occupied = held.astype(F32).astype(BF)
    n = 2 * half
    before = (iota((lanes, lanes), 0) < iota((lanes, lanes), 1)).astype(F32).astype(BF)
    above = (iota((n, n), 1) < iota((n, n), 0)).astype(F32).astype(BF)
    within = nn(occupied, before)
    start = nn(above, nn(occupied, jnp.ones((lanes, lanes), BF)).astype(BF))
    rank = (start + within).astype(jnp.int32)
    last = max(slots // lanes - 1, 0)
    block = jnp.minimum(start.astype(jnp.int32) // lanes, last)
    relative = jnp.where(held, rank - block * lanes, -1)
    count = nt(jnp.ones((8, lanes), BF), occupied).astype(BF)
    below = (iota((n, n), 0) < iota((n, n), 1)).astype(F32).astype(BF)
    start_ref[...] = jnp.minimum(nn(count, below).astype(jnp.int32) // lanes, last)
    for side in range(2):
        at = slice(side * half, (side + 1) * half)
        meta_ref[side, 0] = relative[at].astype(F32)
        meta_ref[side, 1] = q[rows:][at]
        meta_ref[side, 2] = v[rows:][at]


def spot(relative_row, width):
    lanes = relative_row.shape[1]
    ranks = iota((width, lanes), 0).astype(F32)
    return jnp.where(jnp.broadcast_to(relative_row, (width, lanes)) == ranks, 1.0, 0.0).astype(BF)


def edge_rows(x_ref, lo_ref, hi_ref, members, lanes):
    group = 8
    out_row = iota((2 * 2 * group, lanes), 0)
    lane = iota((2 * 2 * group, lanes), 1)
    side = out_row // (2 * group)
    at = out_row - side * 2 * group
    want = at - at // 2 * 2 + side * (lanes - 2)

    def body(g, _):
        total = None
        for i in range(group):
            pick = jnp.where((lane == want) & (at // 2 == i), 1.0, 0.0).astype(BF)
            part = nt(pick, x_ref[g * group + i])
            total = part if total is None else total + part
        total = total.astype(BF)
        at_row = pl.multiple_of(g * 2 * group, 2 * group)
        lo_ref[pl.ds(at_row, 2 * group), :] = total[: 2 * group]
        hi_ref[pl.ds(at_row, 2 * group), :] = total[2 * group :]
        return 0

    lax.fori_loop(0, members // group, body, 0)


def gather_kernel(dims, start_ref, c_ref, e_ref, q_ref, meta_ref,
                  packed_ref, gram_ref, c_lo, c_hi, e_lo, e_hi, wide_ref, sum_ref):
    levels, cols, lanes = dims
    members = e_ref.shape[0]
    half = 2 * levels
    per = 2
    sum_ref[...] = jnp.zeros_like(sum_ref)

    def body(g, gram):
        base = pl.multiple_of(g * per * cols, per * cols)
        wide_ref[...] = e_ref[:, pl.ds(base, per * cols), :].astype(F32).reshape(members * per * cols, lanes)
        weight = q_ref[pl.ds(base, per * cols), :]
        for pair in range(0, per * cols, 2):
            plain, his, los = [], [], []
            for j in (pair, pair + 1):
                x = wide_ref[pl.ds(j, members, stride=per * cols), :]
                xb = x.astype(BF)
                plain.append(xb)
                hi, lo = split(x * weight[j : j + 1])
                his.append(hi)
                los.append(lo)
                col = j % cols
                low, high = col < 2, col >= cols - 2
                for side, here, d in ((0, low, col), (1, high, col - cols + 2)):
                    if not here:
                        continue
                    h = d * levels + g * per + j // cols
                    b = start_ref[0, side * half + h]
                    got = nt(xb, spot(meta_ref[side, 0, pl.ds(h, 1), :], 2 * lanes))
                    sum_ref[b] += got[:, :lanes]
                    sum_ref[b + 1] += got[:, lanes:]
            left = jnp.concatenate([jnp.concatenate(his, axis=1), jnp.concatenate(los, axis=1)], axis=0)
            gram = gram + nt(left, jnp.concatenate(plain, axis=1))
        return gram

    gram = lax.fori_loop(0, levels // per, body, jnp.zeros((2 * members, members), F32))
    gram_ref[...] = gram[:members] + gram[members:]
    blocks = packed_ref.shape[0]
    for b in range(blocks):
        packed_ref[b] = sum_ref[b].astype(BF)
    edge_rows(c_ref, c_lo, c_hi, members, lanes)
    edge_rows(e_ref, e_lo, e_hi, members, lanes)


def exchange_kernel(dims, sizes, taps_ref, c_ref, e_ref, q_ref, v_ref, kf_ref, lf_ref, packed_ref, meta_ref,
                    start_ref, gram_ref, c_lo, c_hi, e_lo, e_hi,
                    p_ref, px_ref, ext_ref, edge_b_ref, edge_a_ref, total_ref,
                    got_ref, got_meta, got_start, start_smem, lat_c, lat_e, lat_x, own_x, outer_ref, inc_ref,
                    wide_ref, send_inc, got_inc, p_edge, got_edge, gram_in,
                    far_sem, far_recv, lat_sem, lat_recv, x_sem, x_recv, inc_sem, inc_recv,
                    pe_sem, pe_recv, gram_sem, gram_recv, smem_sem):
    levels, cols, lanes = dims
    n_lat, n_lon = sizes
    members, rows = c_ref.shape[0], c_ref.shape[1]
    half = 2 * levels
    ext = rows + 2 * half
    lat, lon = lax.axis_index("lat"), lax.axis_index("lon")
    left, right = lax.rem(lon + n_lon - 1, n_lon), lax.rem(lon + 1, n_lon)
    has_before, has_after = lat > 0, lat < n_lat - 1

    def flip(x, bit):
        return x + bit - 2 * bit * (x // bit - x // (2 * bit) * 2)

    partners = [("lat", 1 << i) for i in range(n_lat.bit_length() - 1)]
    partners += [("lon", 1 << i) for i in range(n_lon.bit_length() - 1)]
    barrier = pltpu.get_barrier_semaphore()

    def greet(where):
        pl.semaphore_signal(barrier, inc=1, device_id=where, device_id_type=MESH)

    greet({"lon": left})
    greet({"lon": right})

    @pl.when(has_before)
    def _():
        greet({"lat": lat - 1})

    @pl.when(has_after)
    def _():
        greet({"lat": lat + 1})

    for axis, bit in partners:
        greet({axis: flip(lat if axis == "lat" else lon, bit)})
    pl.semaphore_wait(barrier, 2 + len(partners) + has_before.astype(jnp.int32) + has_after.astype(jnp.int32))

    def remote(src, dst, s, r, where):
        return pltpu.make_async_remote_copy(
            src_ref=src, dst_ref=dst, send_sem=s, recv_sem=r, device_id=where, device_id_type=MESH)

    blocks = packed_ref.shape[0]
    far = []
    for slot, to in ((0, right), (1, left)):
        mine = 1 - slot
        far.append(remote(meta_ref.at[mine], got_meta.at[slot], far_sem.at[slot, 0], far_recv.at[slot, 0], {"lon": to}))
        far.append(remote(start_ref, got_start.at[slot], far_sem.at[slot, 1], far_recv.at[slot, 1], {"lon": to}))
    for slot, to in ((0, right), (1, left)):
        far.append(remote(packed_ref, got_ref.at[slot, pl.ds(0, blocks)], far_sem.at[slot, 2], far_recv.at[slot, 2],
                          {"lon": to}))

    def lat_pairs(lo, hi, dst, s, r, k):
        up = remote(hi, dst.at[0], s.at[0, k], r.at[0, k], {"lat": lat + 1})
        down = remote(lo, dst.at[1], s.at[1, k], r.at[1, k], {"lat": lat - 1})
        return up, down

    def lat_start(pairs):
        for up, down in pairs:
            pl.when(has_after)(up.start)
            pl.when(has_before)(down.start)

    def lat_wait(pairs):
        for up, down in pairs:
            pl.when(has_after)(up.wait_send)
            pl.when(has_before)(down.wait_send)
            pl.when(has_before)(up.wait_recv)
            pl.when(has_after)(down.wait_recv)

    near = [lat_pairs(c_lo, c_hi, lat_c, lat_sem, lat_recv, 0), lat_pairs(e_lo, e_hi, lat_e, lat_sem, lat_recv, 1)]
    lat_start(near)
    for copy in far:
        copy.start()

    @pl.when(jnp.logical_not(has_before))
    def _():
        lat_c[0] = jnp.zeros_like(lat_c[0])
        lat_e[0] = jnp.zeros_like(lat_e[0])
        lat_x[0] = jnp.zeros_like(lat_x[0])
        got_edge[0] = jnp.zeros_like(got_edge[0])

    @pl.when(jnp.logical_not(has_after))
    def _():
        lat_c[1] = jnp.zeros_like(lat_c[1])
        lat_e[1] = jnp.zeros_like(lat_e[1])
        lat_x[1] = jnp.zeros_like(lat_x[1])
        got_edge[1] = jnp.zeros_like(got_edge[1])

    for slot in range(2):
        got_ref[slot, blocks] = jnp.zeros_like(got_ref[slot, blocks])
    inc_ref[...] = jnp.zeros_like(inc_ref)
    total_ref[...] = gram_ref[...]

    def forward(pair, _):
        smooth = []
        for i in range(2):
            x = c_ref[2 * pair + i]
            smooth.append(nn(jnp.concatenate([x, x], axis=1), lf_ref[...]).astype(BF))
        y = jnp.concatenate(smooth, axis=1)
        out = nn(kf_ref[0], y) + nn(kf_ref[1], y)
        total = inc_ref[...]
        for i in range(2):
            m = 2 * pair + i
            part = out[:, i * lanes : (i + 1) * lanes]
            total = total + e_ref[m].astype(F32) * part[:rows]
            outer_ref[m] = part[rows:].astype(BF)
        inc_ref[...] = total
        return 0

    pairs = members // 2
    steps = len(partners) + 1
    cuts = [pairs * i // steps for i in range(steps + 1)]
    for i in range(steps):
        copy = None
        if i < len(partners):
            axis, bit = partners[i]
            gram_in[i, 0] = total_ref[...]
            copy = remote(gram_in.at[i, 0], gram_in.at[i, 1], gram_sem.at[i], gram_recv.at[i],
                          {axis: flip(lat if axis == "lat" else lon, bit)})
            copy.start()
        lax.fori_loop(cuts[i], cuts[i + 1], forward, 0)
        if copy is not None:
            copy.wait()
            total_ref[...] = total_ref[...] + gram_in[i, 1]

    lat_wait(near)
    odd = iota((2 * members, ext), 0) % 2
    mixed = []
    for side in range(2):
        mixed.append(nt(lat_c[side], kf_ref[0]) + nt(lat_c[side], kf_ref[1]))
    edge = [
        taps_ref[0] * mixed[0] + jnp.where(odd == 0, taps_ref[1], 0.0) * pltpu.roll(mixed[0], 2 * members - 1, 0),
        taps_ref[3] * mixed[1] + jnp.where(odd == 1, taps_ref[2], 0.0) * pltpu.roll(mixed[1], 1, 0),
    ]
    edge_lane = iota((8, lanes), 1)
    edge_row = iota((8, lanes), 0)

    def place(e_rows, values):
        out = None
        for side in range(2):
            x = e_rows[side].astype(F32) * values[side]
            x = x.reshape(members // 4, 8, x.shape[1]).sum(axis=0)
            first = side * (lanes - 2)
            pick = jnp.where(edge_lane == first + edge_row % 2, 1.0, 0.0).astype(BF)
            hi, lo = split(x)
            part = tn(hi, pick) + tn(lo, pick)
            out = part if out is None else out + part
        return out

    inc_ref[...] += place((e_lo[...], e_hi[...]), [x[:, :rows] for x in edge])
    edge = [x[:, rows:] for x in edge]

    for copy in far:
        copy.wait()
    for slot in range(2):
        copy = pltpu.make_async_copy(got_start.at[slot], start_smem.at[slot], smem_sem)
        copy.start()
        copy.wait()
    for slot in range(2):
        def expand(h, _, slot=slot):
            b = start_smem[slot, 0, (1 - slot) * half + h]
            hot = spot(got_meta[slot, 0, pl.ds(h, 1), :], 2 * lanes)
            got = nn(jnp.concatenate([got_ref[slot, b], got_ref[slot, b + 1]], axis=1), hot)
            wide_ref[pl.ds(slot * half + h, members, stride=2 * half), :] = got
            return 0

        lax.fori_loop(0, half, expand, 0)

    def outer(m, total):
        at = pl.multiple_of(m * 2 * half, 2 * half)
        x = wide_ref[pl.ds(at, 2 * half), :]
        ext_ref[m] = x.astype(BF)
        return total + x * outer_ref[m].astype(F32)

    given = lax.fori_loop(0, members, outer, jnp.zeros((2 * half, lanes), F32))
    edge_rows(ext_ref, own_x.at[0], own_x.at[1], members, lanes)
    across = [lat_pairs(own_x.at[0], own_x.at[1], lat_x, x_sem, x_recv, 0)]
    lat_start(across)
    given = given + place((own_x[0], own_x[1]), edge)

    for d in range(2):
        at = slice(d * levels, (d + 1) * levels)
        send_inc[0, 0, at] = inc_ref[pl.ds(cols - 2 + d, levels, stride=cols), :]
        send_inc[1, 0, at] = inc_ref[pl.ds(d, levels, stride=cols), :]
    send_inc[0, 1] = given[half:]
    send_inc[1, 1] = given[:half]
    swap = []
    for slot, to in ((0, right), (1, left)):
        swap.append(remote(send_inc.at[slot], got_inc.at[slot], inc_sem.at[slot], inc_recv.at[slot], {"lon": to}))
    for copy in swap:
        copy.start()
    for copy in swap:
        copy.wait()
    for slot in range(2):
        px_ref[slot * half : (slot + 1) * half] = (
            got_meta[slot, 1] * (got_inc[slot, 0] + given[slot * half : (slot + 1) * half]) - got_meta[slot, 2])
        for d in range(2):
            at = pl.ds(slot * (cols - 2) + d, levels, stride=cols)
            inc_ref[at, :] = inc_ref[at, :] + got_inc[slot, 1, d * levels : (d + 1) * levels]
    p_ref[...] = q_ref[...] * inc_ref[...] - v_ref[...]

    want = edge_row % 2 + jnp.where(edge_row < 2, 0, lanes - 2)
    pick = jnp.where((edge_lane == want) & (edge_row < 4), 1.0, 0.0).astype(BF)
    for ref, at in ((p_ref, slice(0, rows)), (px_ref, slice(rows, ext))):
        hi, lo = split(ref[...])
        p_edge[:, at] = nt(pick, hi) + nt(pick, lo)
    last = [lat_pairs(p_edge, p_edge, got_edge, pe_sem, pe_recv, 0)]
    lat_start(last)
    lat_wait(across)
    lat_wait(last)
    for side, out_ref in ((0, edge_b_ref), (1, edge_a_ref)):
        first = 2 - 2 * side
        got = got_edge[side]
        p = jnp.where(odd == 0, got[first : first + 1], got[first + 1 : first + 2])
        e = jnp.concatenate([lat_e[side], lat_x[side]], axis=1)
        out_ref[...] = (e.astype(F32) * p).astype(BF)


def adjoint_kernel(dims, block, taps_ref, c_ref, e_ref, ext_ref, p_ref, px_ref, edge_b_ref, edge_a_ref, ka_ref,
                   la_ref, out_ref, edge_ref):
    levels, cols, lanes = dims
    members, rows = c_ref.shape[0], c_ref.shape[1]
    step = pl.program_id(0)
    per = lanes // 4

    @pl.when(step == 0)
    def _():
        groups = edge_ref.shape[0]
        shape = (2 * members, groups * lanes)
        src, dst = iota(shape, 0), iota(shape, 1)
        same = src // 2 == dst // 4
        u, t = src % 2, dst % 4
        total = jnp.zeros((rows, groups * lanes), F32)
        for side, ref in ((0, edge_b_ref), (1, edge_a_ref)):
            z = (nt(ka_ref[0], ref[...]) + nt(ka_ref[1], ref[...])).astype(BF)
            if side == 0:
                w = jnp.where(t == u + 2, taps_ref[3], 0.0) + jnp.where((t == 2) & (u == 1), taps_ref[2], 0.0)
            else:
                w = jnp.where(t == u, taps_ref[0], 0.0) + jnp.where((t == 1) & (u == 0), taps_ref[1], 0.0)
            for part in split(jnp.where(same, w, 0.0)):
                total = total + nn(z, part)
        for g in range(groups):
            edge_ref[g] = total[:, g * lanes : (g + 1) * lanes]

    lane = iota((rows, lanes), 1)
    at_edge = (lane < 2) | (lane >= lanes - 2)
    p, px = p_ref[...], px_ref[...]

    for pair in range(block // 2):
        wide = []
        for i in range(2):
            m = step * block + 2 * pair + i
            own = (e_ref[m].astype(F32) * p).astype(BF)
            far = (ext_ref[m].astype(F32) * px).astype(BF)
            wide.append(jnp.concatenate([own, far], axis=0))
        wide = jnp.concatenate(wide, axis=1)
        z = (nn(ka_ref[0], wide) + nn(ka_ref[1], wide)).astype(BF)
        for i in range(2):
            m = step * block + 2 * pair + i
            zi = z[:, i * lanes : (i + 1) * lanes]
            y = nn(jnp.concatenate([zi, zi], axis=1), la_ref[...])
            g = m // per
            turned = pltpu.roll(edge_ref[g], lax.rem(2 * lanes - 2 - 4 * (m - g * per), lanes), 1)
            out_ref[2 * pair + i] = c_ref[m].astype(F32) + y + jnp.where(at_edge, turned, 0.0)


def shards(
    control, ensemble, level_mix, lat_taps, lon_taps, obs_location, obs_count, obs_keep, innovation, obs_weight
):
    members, levels, cols, lanes = control.shape
    dims = (levels, cols, lanes)
    rows, half = levels * cols, 2 * levels
    ext = rows + 2 * half
    slots = obs_location.shape[2]
    blocks = slots // lanes
    n_lat, n_lon = lax.axis_size("lat"), lax.axis_size("lon")
    vm, sm = pl.BlockSpec(memory_space=pltpu.VMEM), pl.BlockSpec(memory_space=pltpu.SMEM)
    here = functools.partial(pltpu.with_memory_space_constraint, memory_space=pltpu.VMEM)
    e3 = here(ensemble.reshape(members, rows, lanes))
    c3 = here(control.reshape(members, rows, lanes))
    taps = jnp.concatenate([lat_taps, lon_taps])

    def sds(shape, dtype=F32):
        return jax.ShapeDtypeStruct(shape, dtype)

    kf, ka, lf, la, q, v, meta, start = pl.pallas_call(
        functools.partial(setup_kernel, dims),
        in_specs=[sm, sm] + [vm] * 5,
        out_specs=[vm] * 8,
        out_shape=[sds((2, ext, rows), BF), sds((2, rows, ext), BF), sds((2 * lanes, lanes), BF),
                   sds((2 * lanes, lanes), BF), sds((rows, lanes)), sds((rows, lanes)),
                   sds((2, 3, half, lanes)), sds((8, 2 * half), jnp.int32)],
        compiler_params=pltpu.CompilerParams(vmem_limit_bytes=8 * MIB),
        name="setup",
    )(taps, obs_count, level_mix, obs_location[0], obs_keep[0], obs_weight[0], innovation[0])

    edges = [sds((2 * members, rows), BF)] * 4
    packed, gram, c_lo, c_hi, e_lo, e_hi = pl.pallas_call(
        functools.partial(gather_kernel, dims),
        in_specs=[sm] + [vm] * 4,
        out_specs=[vm] * 6,
        out_shape=[sds((blocks, members, lanes), BF), sds((members, members))] + edges,
        scratch_shapes=[pltpu.VMEM((members * 2 * cols, lanes), F32),
                        pltpu.VMEM((blocks + 1, members, lanes), F32)],
        compiler_params=pltpu.CompilerParams(vmem_limit_bytes=12 * MIB),
        name="gather",
    )(start, c3, e3, q, meta)

    n_bits = (n_lat.bit_length() - 1) + (n_lon.bit_length() - 1)
    dma = pltpu.SemaphoreType.DMA
    p, px, e_ext, edge_b, edge_a, gram = pl.pallas_call(
        functools.partial(exchange_kernel, dims, (n_lat, n_lon)),
        in_specs=[sm] + [vm] * 14,
        out_specs=[vm] * 6,
        out_shape=[sds((rows, lanes)), sds((2 * half, lanes)), sds((members, 2 * half, lanes), BF),
                   sds((2 * members, ext), BF), sds((2 * members, ext), BF), sds((members, members))],
        scratch_shapes=[
            pltpu.VMEM((2, blocks + 1, members, lanes), BF),
            pltpu.VMEM((2, 3, half, lanes), F32),
            pltpu.VMEM((2, 8, 2 * half), jnp.int32),
            pltpu.SMEM((2, 8, 2 * half), jnp.int32),
            pltpu.VMEM((2, 2 * members, rows), BF),
            pltpu.VMEM((2, 2 * members, rows), BF),
            pltpu.VMEM((2, 2 * members, 2 * half), BF),
            pltpu.VMEM((2, 2 * members, 2 * half), BF),
            pltpu.VMEM((members, 2 * half, lanes), BF),
            pltpu.VMEM((rows, lanes), F32),
            pltpu.VMEM((members * 2 * half, lanes), F32),
            pltpu.VMEM((2, 2, half, lanes), F32),
            pltpu.VMEM((2, 2, half, lanes), F32),
            pltpu.VMEM((8, ext), F32),
            pltpu.VMEM((2, 8, ext), F32),
            pltpu.VMEM((n_bits, 2, members, members), F32),
            dma((2, 3)), dma((2, 3)), dma((2, 2)), dma((2, 2)), dma((2, 1)), dma((2, 1)), dma((2,)), dma((2,)),
            dma((2, 1)), dma((2, 1)), dma((n_bits,)), dma((n_bits,)), dma,
        ],
        compiler_params=pltpu.CompilerParams(
            vmem_limit_bytes=14 * MIB, collective_id=0, has_side_effects=True),
        name="exchange",
    )(taps, c3, e3, q, v, kf, lf, packed, meta, start, gram, c_lo, c_hi, e_lo, e_hi)

    block = 8 if members % 8 == 0 else 2
    groups = -(-4 * members // lanes)
    gradient = pl.pallas_call(
        functools.partial(adjoint_kernel, dims, block),
        grid=(members // block,),
        in_specs=[sm] + [vm] * 9,
        out_specs=pl.BlockSpec((block, rows, lanes), lambda g: (g, 0, 0)),
        out_shape=sds((members, rows, lanes)),
        scratch_shapes=[pltpu.VMEM((groups, rows, lanes), F32)],
        compiler_params=pltpu.CompilerParams(vmem_limit_bytes=8 * MIB),
        name="adjoint",
    )(taps, c3, e3, e_ext, p, px, edge_b, edge_a, ka, la)
    total_obs = slots * n_lat * n_lon
    upper = jnp.linalg.cholesky(jnp.eye(members, dtype=F32) + members / total_obs * gram).T
    return gradient.reshape(members, levels, cols, lanes), upper


def solution(mesh):
    in_specs = (
        P(None, None, "lon", "lat"),
        P(None, None, "lon", "lat"),
        P(),
        P(),
        P(),
        P("lon", "lat", None),
        P("lon", "lat"),
        P("lon", "lat", None),
        P("lon", "lat", None),
        P("lon", "lat", None),
    )
    out_specs = (P(None, None, "lon", "lat"), P())
    return jax.shard_map(shards, mesh=mesh, in_specs=in_specs, out_specs=out_specs, check_vma=False)
```

```python
import functools

import jax
import jax.numpy as jnp
from jax import lax
from jax.experimental import pallas as pl
from jax.experimental.pallas import tpu as pltpu
from jax.sharding import PartitionSpec as P

OFFSETS = (-2, -1, 1, 2)
F32, BF = jnp.float32, jnp.bfloat16
MIB = 1024 * 1024
MESH = pl.DeviceIdType.MESH


def nn(a, b):
    return jnp.dot(a, b, preferred_element_type=F32)


def nt(a, b):
    return lax.dot_general(a, b, (((1,), (1,)), ((), ())), preferred_element_type=F32)


def tn(a, b):
    return lax.dot_general(a, b, (((0,), (0,)), ((), ())), preferred_element_type=F32)


def split(x):
    hi = x.astype(BF)
    return hi, (x - hi.astype(F32)).astype(BF)


def iota(shape, axis):
    return lax.broadcasted_iota(jnp.int32, shape, axis)


def band(diff, taps_ref, sign):
    out = jnp.where(diff == 0, 1.0, 0.0)
    for t, offset in enumerate(OFFSETS):
        out = out + jnp.where(diff == sign * offset, taps_ref[t], 0.0)
    return out


def halo_place(h, levels, cols):
    side = h // (2 * levels)
    rest = h - side * 2 * levels
    d = rest // levels
    return rest - d * levels, d + side * (cols - 2), d - 2 + side * (cols + 2)


def setup_kernel(dims, lat_taps, lon_taps, count_ref, e_hbm, mix_hbm, place_hbm, keep_hbm, weight_hbm, innov_hbm,
                 e_ref, kf_ref, ka_ref, lf_ref, la_ref, bf_ref, ba_ref, q_ref, v_ref, meta_ref, start_ref,
                 mix_ref, place_ref, keep_ref, weight_ref, innov_ref, sems):
    levels, cols, lanes = dims
    small = [pltpu.make_async_copy(a, b, sems.at[i]) for i, (a, b) in enumerate(
        ((mix_hbm, mix_ref), (place_hbm, place_ref), (keep_hbm, keep_ref), (weight_hbm, weight_ref),
         (innov_hbm, innov_ref)))]
    large = pltpu.make_async_copy(e_hbm, e_ref, sems.at[5])
    for copy in small:
        copy.start()
    large.start()
    rows, half = levels * cols, 2 * levels
    ext = rows + 2 * half

    def ext_level_col(x):
        k, own, outer = halo_place(x - rows, levels, cols)
        inside = x < rows
        xk = x // cols
        return jnp.where(inside, xk, k), jnp.where(inside, x - xk * cols, own), jnp.where(
            inside, x - xk * cols, outer)

    diff = iota((lanes, lanes), 0) - iota((lanes, lanes), 1)
    lf_ref[...] = jnp.concatenate(split(band(diff, lat_taps, 1)), axis=0)
    la_ref[...] = jnp.concatenate(split(band(diff, lat_taps, -1)), axis=0)
    src, dst = iota((lanes, lanes), 0), iota((lanes, lanes), 1)
    member = (src // 4) == (dst // 4)
    t, u = src % 4, dst % 4
    at = jnp.where(t < 2, t - 2, lanes + t - 2) - jnp.where(u < 2, lanes - 2 + u, u - 2)
    bf_ref[...] = jnp.concatenate(split(jnp.where(member, band(at, lat_taps, 1), 0.0)), axis=0)
    ba_ref[...] = jnp.concatenate(split(jnp.where(member, band(at, lat_taps, -1), 0.0)), axis=0)
    for copy in small:
        copy.wait()
    mix = mix_ref[...]
    level, _, col = ext_level_col(iota((ext, rows), 0))
    y = iota((ext, rows), 1)
    taps = band((y - y // cols * cols) - col, lon_taps, 1)
    pick = (ext_level_col(iota((ext, levels), 0))[0] == iota((ext, levels), 1)).astype(F32).astype(BF)
    put = (iota((levels, rows), 1) // cols == iota((levels, rows), 0)).astype(F32).astype(BF)
    hi, lo = split(nn(nn(pick, mix).astype(BF), put) * taps)
    kf_ref[:ext] = hi
    kf_ref[ext:] = lo
    level, _, col = ext_level_col(iota((rows, ext), 1))
    y = iota((rows, ext), 0)
    taps = band((y - y // cols * cols) - col, lon_taps, 1)
    pick = (ext_level_col(iota((levels, ext), 1))[0] == iota((levels, ext), 0)).astype(F32).astype(BF)
    put = (iota((rows, levels), 0) // cols == iota((rows, levels), 1)).astype(F32).astype(BF)
    hi, lo = split(nn(put, nn(mix.T, pick).astype(BF)) * taps)
    ka_ref[:rows] = hi
    ka_ref[rows:] = lo
    slots = place_ref.shape[1]
    chunk = 512 if slots % 512 == 0 else slots
    ids = iota((ext, chunk), 0)
    ids_level, ids_col, _ = ext_level_col(iota((ext, 1), 0))
    ids = jnp.broadcast_to(ids_level * cols + ids_col, (ext, chunk))
    lane_ids = iota((lanes, chunk), 0)
    total = jnp.zeros((ext, 4 * lanes), F32)
    for s in range(0, slots, chunk):
        place = place_ref[:, s : s + chunk]
        r = place // lanes
        c = place - r * lanes
        live = (iota((1, chunk), 1) + s < count_ref[0, 0]).astype(F32) * keep_ref[:, s : s + chunk].astype(F32)
        q = live * weight_ref[:, s : s + chunk]
        v = q * innov_ref[:, s : s + chunk]
        hit = lane_ids == c
        parts = []
        for x in (q, v):
            for part in split(x):
                parts.append(jnp.where(hit, part.astype(F32), 0.0).astype(BF))
        total = total + nt((ids == r).astype(F32).astype(BF), jnp.concatenate(parts, axis=0))
    q = total[:, :lanes] + total[:, lanes : 2 * lanes]
    v = total[:, 2 * lanes : 3 * lanes] + total[:, 3 * lanes :]
    q_ref[...] = q[:rows]
    v_ref[...] = v[:rows]
    held = q[rows:] > 0.0
    occupied = held.astype(F32).astype(BF)
    n = 2 * half
    before = (iota((lanes, lanes), 0) < iota((lanes, lanes), 1)).astype(F32).astype(BF)
    above = (iota((n, n), 1) < iota((n, n), 0)).astype(F32).astype(BF)
    within = nn(occupied, before)
    start = nn(above, nn(occupied, jnp.ones((lanes, lanes), BF)).astype(BF))
    rank = (start + within).astype(jnp.int32)
    last = max(slots // lanes - 1, 0)
    block = jnp.minimum(start.astype(jnp.int32) // lanes, last)
    relative = jnp.where(held, rank - block * lanes, -1)
    count = nt(jnp.ones((8, lanes), BF), occupied).astype(BF)
    below = (iota((n, n), 0) < iota((n, n), 1)).astype(F32).astype(BF)
    start_ref[...] = jnp.minimum(nn(count, below).astype(jnp.int32) // lanes, last)
    for side in range(2):
        at = slice(side * half, (side + 1) * half)
        meta_ref[side, 0] = relative[at].astype(F32)
        meta_ref[side, 1] = q[rows:][at]
        meta_ref[side, 2] = v[rows:][at]
    large.wait()


def spot(relative_row, width):
    lanes = relative_row.shape[1]
    ranks = iota((width, lanes), 0).astype(F32)
    return jnp.where(jnp.broadcast_to(relative_row, (width, lanes)) == ranks, 1.0, 0.0).astype(BF)


def turn_edges(x, m, at_edge):
    lanes = x.shape[1]
    per = lanes // 4
    return pltpu.roll(jnp.where(at_edge, x, 0.0), lax.rem(2 + 4 * (m - m // per * per), lanes), 1)


def load_rows(ref, j, members, stride):
    return ref[pl.ds(j, members, stride=stride), :]


def gather_kernel(dims, start_ref, c_hbm, e_ref, meta_ref, c_ref, packed_ref, wide_ref, sum_ref, sem):
    levels, cols, lanes = dims
    members = e_ref.shape[0]
    half = 2 * levels
    per = 2
    pitch = per * cols + 8
    copy = pltpu.make_async_copy(c_hbm, c_ref, sem)
    copy.start()
    sum_ref[...] = jnp.zeros_like(sum_ref)

    def body(g, _):
        base = pl.multiple_of(g * per * cols, per * cols)
        x = e_ref[:, pl.ds(base, per * cols), :].astype(F32)
        for m in range(members):
            wide_ref[m * pitch : m * pitch + per * cols, :] = x[m]
        found = []
        for j in range(per * cols):
            col = j % cols
            if 2 <= col < cols - 2:
                continue
            side = int(col >= 2)
            h = (col - side * (cols - 2)) * levels + g * per + j // cols
            xb = load_rows(wide_ref, j, members, pitch).astype(BF)
            got = nt(xb, spot(meta_ref[side, 0, pl.ds(h, 1), :], 2 * lanes))
            found.append((start_ref[0, side * half + h], got))
        for b, got in found:
            sum_ref[b] += got[:, :lanes]
            sum_ref[b + 1] += got[:, lanes:]
        return 0

    lax.fori_loop(0, levels // per, body, 0)
    for b in range(packed_ref.shape[0]):
        packed_ref[b] = sum_ref[b].astype(BF)
    copy.wait()


def factor(s_ref, out_ref, size):
    lanes = s_ref.shape[1]
    step = 8
    lane = iota((step, lanes), 1)
    row = iota((step, lanes), 0)
    for b in range(0, size, step):
        panel = s_ref[b : b + step, :]
        cols = [jnp.broadcast_to(panel[:, b + i : b + i + 1], (step, lanes)) for i in range(step)]
        done = jnp.zeros((step, lanes), F32)
        for j in range(step):
            scale = lax.rsqrt(jnp.broadcast_to(cols[j][j : j + 1], (step, lanes)))
            across = jnp.broadcast_to(panel[j : j + 1], (step, lanes)) * scale
            done = jnp.where(row == j, across, done)
            down = cols[j] * scale
            panel = panel - down * across
            for i in range(j + 1, step):
                cols[i] = cols[i] - down * jnp.broadcast_to(down[i : i + 1], (step, lanes))
        done = jnp.where(lane >= b + row, done, 0.0)
        out_ref[b : b + step, :] = done[:, :size]
        if b + step < size:
            hi, lo = split(done)
            low = jnp.concatenate([hi, hi, lo], axis=0)
            high = jnp.concatenate([hi, lo, hi], axis=0)
            s_ref[...] = s_ref[...] - tn(low, high)[:size]


def exchange_kernel(dims, sizes, lat_taps, c_ref, e_ref, q_ref, v_ref, kf_ref, lf_ref, bf_ref, packed_ref, meta_ref,
                    start_ref,
                    p_ref, px_ref, ext_ref, edge_ref, upper_ref,
                    got_left, got_right, got_meta, got_start, start_smem, own_c, own_e, lat_c, lat_e, lat_x, own_x, outer_ref,
                    inc_ref, wide_ref, send_inc, got_inc, p_edge, got_edge, gram_in, total_ref, given_ref,
                    far_sem, far_recv, lat_sem, lat_recv, x_sem, x_recv, inc_sem, inc_recv,
                    pe_sem, pe_recv, gram_sem, gram_recv, smem_sem):
    levels, cols, lanes = dims
    n_lat, n_lon = sizes
    members, rows = c_ref.shape[0], c_ref.shape[1]
    half = 2 * levels
    ext = rows + 2 * half
    per = lanes // 4
    groups = own_e.shape[0]
    lat, lon = lax.axis_index("lat"), lax.axis_index("lon")
    left, right = lax.rem(lon + n_lon - 1, n_lon), lax.rem(lon + 1, n_lon)
    has_before, has_after = lat > 0, lat < n_lat - 1

    def flip(x, bit):
        return x + bit - 2 * bit * (x // bit - x // (2 * bit) * 2)

    partners = [("lat", 1 << i) for i in range(n_lat.bit_length() - 1)]
    n_near = len(partners)
    partners += [("lon", 1 << i) for i in range(n_lon.bit_length() - 1)]
    barrier = pltpu.get_barrier_semaphore()

    def greet(where):
        pl.semaphore_signal(barrier, inc=1, device_id=where, device_id_type=MESH)

    greet({"lon": left})
    greet({"lon": right})

    @pl.when(has_before)
    def _():
        greet({"lat": lat - 1})

    @pl.when(has_after)
    def _():
        greet({"lat": lat + 1})

    for axis, bit in partners:
        greet({axis: flip(lat if axis == "lat" else lon, bit)})

    lane = iota((rows, lanes), 1)
    at_edge = (lane < 2) | (lane >= lanes - 2)
    for g in range(groups):
        first, last = g * per, min((g + 1) * per, members)

        def pack(k, both, first=first):
            c, e = both
            for i in range(2):
                m = first + 2 * k + i
                c = c + turn_edges(c_ref[m].astype(F32), m, at_edge)
                e = e + turn_edges(e_ref[m].astype(F32), m, at_edge)
            return c, e

        zero = jnp.zeros((rows, lanes), F32)
        c, e = lax.fori_loop(0, (last - first) // 2, pack, (zero, zero))
        own_c[g] = c.astype(BF)
        own_e[g] = e.astype(BF)

    pl.semaphore_wait(barrier, 2 + len(partners) + has_before.astype(jnp.int32) + has_after.astype(jnp.int32))

    def remote(src, dst, s, r, where):
        return pltpu.make_async_remote_copy(
            src_ref=src, dst_ref=dst, send_sem=s, recv_sem=r, device_id=where, device_id_type=MESH)

    blocks = packed_ref.shape[0]
    got = (got_left, got_right)
    far = []
    for slot, to in ((0, right), (1, left)):
        mine = 1 - slot
        far.append([
            remote(meta_ref.at[mine], got_meta.at[slot], far_sem.at[slot, 0], far_recv.at[slot, 0], {"lon": to}),
            remote(start_ref, got_start.at[slot], far_sem.at[slot, 1], far_recv.at[slot, 1], {"lon": to}),
            remote(packed_ref, got[slot].at[pl.ds(0, blocks)], far_sem.at[slot, 2], far_recv.at[slot, 2],
                   {"lon": to})])

    def lat_pair(src, dst, s, r, k):
        up = remote(src, dst.at[0], s.at[0, k], r.at[0, k], {"lat": lat + 1})
        down = remote(src, dst.at[1], s.at[1, k], r.at[1, k], {"lat": lat - 1})
        return up, down

    def lat_start(up, down):
        pl.when(has_after)(up.start)
        pl.when(has_before)(down.start)

    def lat_wait(up, down):
        pl.when(has_after)(up.wait_send)
        pl.when(has_before)(down.wait_send)
        pl.when(has_before)(up.wait_recv)
        pl.when(has_after)(down.wait_recv)

    near = [lat_pair(own_c, lat_c, lat_sem, lat_recv, 0), lat_pair(own_e, lat_e, lat_sem, lat_recv, 1)]
    for pair in near:
        lat_start(*pair)
    for copies in far:
        for copy in copies:
            copy.start()

    for side, missing in ((0, jnp.logical_not(has_before)), (1, jnp.logical_not(has_after))):
        @pl.when(missing)
        def _(side=side):
            for ref in (lat_c, lat_e, lat_x, got_edge):
                ref[side] = jnp.zeros_like(ref[side])

    for slot in range(2):
        got[slot][blocks] = jnp.zeros_like(got[slot][blocks])
    inc_ref[...] = jnp.zeros_like(inc_ref)

    two = 2
    pitch = two * cols + 8

    def grams(g, gram):
        base = pl.multiple_of(g * two * cols, two * cols)
        x = e_ref[:, pl.ds(base, two * cols), :].astype(F32)
        for m in range(members):
            wide_ref[m * pitch : m * pitch + two * cols, :] = x[m]
        weight = q_ref[pl.ds(base, two * cols), :]
        for pair in range(0, two * cols, 2):
            plain, his, los = [], [], []
            for j in (pair, pair + 1):
                y = load_rows(wide_ref, j, members, pitch)
                plain.append(y.astype(BF))
                hi, lo = split(y * weight[j : j + 1])
                his.append(hi)
                los.append(lo)
            weighted = jnp.concatenate([jnp.concatenate(his, axis=1), jnp.concatenate(los, axis=1)], axis=0)
            gram = gram + nt(weighted, jnp.concatenate(plain, axis=1))
        return gram

    gram = lax.fori_loop(0, levels // two, grams, jnp.zeros((2 * members, members), F32))
    total_ref[...] = jnp.zeros_like(total_ref)
    total_ref[:, :members] = gram[:members] + gram[members:]

    stages = []

    def stage_start():
        i = len(stages)
        if i < len(partners):
            axis, bit = partners[i]
            gram_in[i, 0] = total_ref[...]
            copy = remote(gram_in.at[i, 0], gram_in.at[i, 1], gram_sem.at[i], gram_recv.at[i],
                          {axis: flip(lat if axis == "lat" else lon, bit)})
            copy.start()
            stages.append(copy)

    def stage_end():
        i = len(stages) - 1
        stages[i].wait()
        total_ref[...] = total_ref[...] + gram_in[i, 1]

    def forward(pair, _):
        x = [c_ref[2 * pair + i] for i in range(2)]
        x = jnp.concatenate([jnp.concatenate([y, y], axis=1) for y in x], axis=0)
        y = nn(x, lf_ref[...]).astype(BF)
        out = nn(kf_ref[...], jnp.concatenate([y[:rows], y[rows:]], axis=1))
        out = out[:ext] + out[ext:]
        total = inc_ref[...]
        for i in range(2):
            m = 2 * pair + i
            part = out[:, i * lanes : (i + 1) * lanes]
            total = total + e_ref[m].astype(F32) * part[:rows]
            outer_ref[m] = part[rows:].astype(BF)
        inc_ref[...] = total
        return 0

    pairs = members // 2
    cuts = [pairs * i // (n_near + 1) for i in range(n_near + 2)]
    for i in range(n_near + 1):
        stage_start()
        lax.fori_loop(cuts[i], cuts[i + 1], forward, 0)
        if i < n_near:
            stage_end()

    for pair in near:
        lat_wait(*pair)
    before = iota((rows, lanes), 1) % 4 < 2
    spare = []
    for g in range(groups):
        halo = jnp.where(before, lat_c[0, g].astype(F32), lat_c[1, g].astype(F32)).astype(BF)
        mixed = nn(kf_ref[...], halo)
        mixed = (mixed[:ext] + mixed[ext:]).astype(BF)
        spare.append(nn(jnp.concatenate([mixed, mixed], axis=1), bf_ref[...]))
    source = iota((lanes, lanes), 0) % 4
    target = iota((lanes, lanes), 1)
    drop = (target == jnp.where(source < 2, lanes - 2 + source, source - 2)).astype(F32).astype(BF)

    def settle(products):
        total = None
        for x in products:
            part = nn(jnp.concatenate(split(x), axis=1), jnp.concatenate([drop, drop], axis=0))
            total = part if total is None else total + part
        return total

    inc_ref[...] += settle([own_e[g].astype(F32) * spare[g][:rows] for g in range(groups)])

    pitch_x = 2 * half + 8
    for slot in range(2):
        for copy in far[slot]:
            copy.wait()
        copy = pltpu.make_async_copy(got_start.at[slot], start_smem.at[slot], smem_sem)
        copy.start()
        copy.wait()

        def expand(k, _, slot=slot):
            for i in range(8):
                h = k * 8 + i
                b = start_smem[slot, 0, (1 - slot) * half + h]
                hot = spot(got_meta[slot, 0, pl.ds(h, 1), :], 2 * lanes)
                x = nn(jnp.concatenate([got[slot][b], got[slot][b + 1]], axis=1), hot)
                wide_ref[pl.ds(slot * half + h, members, stride=pitch_x), :] = x
            return 0

        lax.fori_loop(0, half // 8, expand, 0)
        if len(stages) > n_near:
            stage_end()
            stage_start()

    edge_x = at_edge[: 2 * half]
    given_ref[...] = jnp.zeros_like(given_ref)
    for g in range(groups):
        first, last = g * per, min((g + 1) * per, members)

        def outer(k, carry, first=first):
            total, edges = carry
            for i in range(2):
                m = first + 2 * k + i
                x = wide_ref[pl.ds(pl.multiple_of(m * pitch_x, 8), 2 * half), :]
                ext_ref[m] = x.astype(BF)
                total = total + x * outer_ref[m].astype(F32)
                edges = edges + turn_edges(x, m, edge_x)
            return total, edges

        zero = jnp.zeros((2 * half, lanes), F32)
        total, edges = lax.fori_loop(0, (last - first) // 2, outer, (zero, zero))
        given_ref[...] += total
        own_x[g] = edges.astype(BF)
    given_ref[...] += settle([own_x[g].astype(F32) * spare[g][rows:] for g in range(groups)])

    for d in range(2):
        at = slice(d * levels, (d + 1) * levels)
        send_inc[0, 0, at] = inc_ref[pl.ds(cols - 2 + d, levels, stride=cols), :]
        send_inc[1, 0, at] = inc_ref[pl.ds(d, levels, stride=cols), :]
    send_inc[0, 1] = given_ref[half:]
    send_inc[1, 1] = given_ref[:half]
    swap = []
    for slot, to in ((0, right), (1, left)):
        swap.append(remote(send_inc.at[slot], got_inc.at[slot], inc_sem.at[slot], inc_recv.at[slot], {"lon": to}))
    for copy in swap:
        copy.start()
    across = lat_pair(own_x, lat_x, x_sem, x_recv, 0)
    lat_start(*across)

    while True:
        if stages:
            stage_end()
        if len(stages) == len(partners):
            break
        stage_start()
    eye = (iota((members, lanes), 0) == iota((members, lanes), 1)).astype(F32)
    total_obs = packed_ref.shape[0] * lanes * n_lat * n_lon
    total_ref[...] = eye + members / total_obs * total_ref[...]
    factor(total_ref, upper_ref, members)

    for copy in swap:
        copy.wait()
    for slot in range(2):
        px_ref[slot * half : (slot + 1) * half] = (
            got_meta[slot, 1] * (got_inc[slot, 0] + given_ref[slot * half : (slot + 1) * half]) - got_meta[slot, 2])
        for d in range(2):
            at = pl.ds(slot * (cols - 2) + d, levels, stride=cols)
            inc_ref[at, :] = inc_ref[at, :] + got_inc[slot, 1, d * levels : (d + 1) * levels]
    p_ref[...] = q_ref[...] * inc_ref[...] - v_ref[...]

    edge_row, edge_lane = iota((8, lanes), 0), iota((8, lanes), 1)
    pick = jnp.where(edge_lane == jnp.where(edge_row < 2, lanes - 2 + edge_row, edge_row - 2), 1.0, 0.0)
    pick = jnp.where(edge_row < 4, pick, 0.0).astype(BF)
    for ref, at in ((p_ref, slice(0, rows)), (px_ref, slice(rows, ext))):
        hi, lo = split(ref[...])
        p_edge[:, at] = nt(pick, hi) + nt(pick, lo)
    final = lat_pair(p_edge, got_edge, pe_sem, pe_recv, 0)
    lat_start(*final)
    lat_wait(*across)
    before = iota((ext, lanes), 1) % 4 < 2
    halo = []
    for g in range(groups):
        far_e = [jnp.concatenate([lat_e[side, g], lat_x[side, g]], axis=0).astype(F32) for side in range(2)]
        halo.append(jnp.where(before, far_e[0], far_e[1]))
    spread = jnp.where((edge_lane % 4 == edge_row) & (edge_row < 4), 1.0, 0.0).astype(BF)
    lat_wait(*final)
    p_halo = jnp.where(iota((8, ext), 0) < 2, got_edge[0], got_edge[1])
    hi, lo = split(p_halo)
    p_halo = tn(hi, spread) + tn(lo, spread)
    for g in range(groups):
        edge_ref[g] = (halo[g] * p_halo).astype(BF)


def adjoint_kernel(dims, block, c_ref, e_ref, ext_ref, p_ref, px_ref, pe_ref, ka_ref, la_ref, ba_ref, upper_ref,
                   out_ref, upper_out, edge_ref):
    levels, cols, lanes = dims
    members, rows = c_ref.shape[0], c_ref.shape[1]
    step = pl.program_id(0)
    per = lanes // 4

    @pl.when(step == 0)
    def _():
        upper_out[...] = upper_ref[...]
        for g in range(edge_ref.shape[0]):
            z = nn(ka_ref[...], pe_ref[g])
            z = (z[:rows] + z[rows:]).astype(BF)
            edge_ref[g] = nn(jnp.concatenate([z, z], axis=1), ba_ref[...])

    lane = iota((rows, lanes), 1)
    at_edge = (lane < 2) | (lane >= lanes - 2)
    p, px = p_ref[...], px_ref[...]

    for pair in range(block // 2):
        wide = []
        for i in range(2):
            m = step * block + 2 * pair + i
            own = (e_ref[m].astype(F32) * p).astype(BF)
            far = (ext_ref[m].astype(F32) * px).astype(BF)
            wide.append(jnp.concatenate([own, far], axis=0))
        z = nn(ka_ref[...], jnp.concatenate(wide, axis=1))
        z = (z[:rows] + z[rows:]).astype(BF)
        z = jnp.concatenate([z[:, :lanes], z[:, lanes:]], axis=0)
        y = nn(jnp.concatenate([z, z], axis=1), la_ref[...])
        for i in range(2):
            m = step * block + 2 * pair + i
            g = m // per
            turned = pltpu.roll(edge_ref[g], lax.rem(2 * lanes - 2 - 4 * (m - g * per), lanes), 1)
            out_ref[2 * pair + i] = (
                c_ref[m].astype(F32) + y[i * rows : (i + 1) * rows] + jnp.where(at_edge, turned, 0.0))


def shards(
    control, ensemble, level_mix, lat_taps, lon_taps, obs_location, obs_count, obs_keep, innovation, obs_weight
):
    members, levels, cols, lanes = control.shape
    dims = (levels, cols, lanes)
    rows, half = levels * cols, 2 * levels
    ext = rows + 2 * half
    slots = obs_location.shape[2]
    blocks = slots // lanes
    groups = -(-4 * members // lanes)
    n_lat, n_lon = lax.axis_size("lat"), lax.axis_size("lon")
    vm, sm = pl.BlockSpec(memory_space=pltpu.VMEM), pl.BlockSpec(memory_space=pltpu.SMEM)
    hbm = pl.BlockSpec(memory_space=pltpu.HBM)
    dma = pltpu.SemaphoreType.DMA
    away = functools.partial(pltpu.with_memory_space_constraint, memory_space=pltpu.HBM)

    def sds(shape, dtype=F32):
        return jax.ShapeDtypeStruct(shape, dtype)

    e3, kf, ka, lf, la, bf, ba, q, v, meta, start = pl.pallas_call(
        functools.partial(setup_kernel, dims),
        in_specs=[sm, sm, sm] + [hbm] * 6,
        out_specs=[vm] * 11,
        out_shape=[sds((members, rows, lanes), BF), sds((2 * ext, rows), BF), sds((2 * rows, ext), BF)]
        + [sds((2 * lanes, lanes), BF)] * 4
        + [sds((rows, lanes)), sds((rows, lanes)), sds((2, 3, half, lanes)), sds((8, 2 * half), jnp.int32)],
        scratch_shapes=[pltpu.VMEM((levels, levels), BF), pltpu.VMEM((1, slots), jnp.int32),
                        pltpu.VMEM((1, slots), jnp.int32), pltpu.VMEM((1, slots), F32), pltpu.VMEM((1, slots), F32),
                        dma((6,))],
        compiler_params=pltpu.CompilerParams(vmem_limit_bytes=8 * MIB),
        name="setup",
    )(lat_taps, lon_taps, obs_count, away(ensemble.reshape(members, rows, lanes)), away(level_mix),
      away(obs_location[0]), away(obs_keep[0]), away(obs_weight[0]), away(innovation[0]))

    c3, packed = pl.pallas_call(
        functools.partial(gather_kernel, dims),
        in_specs=[sm, hbm, vm, vm],
        out_specs=[vm] * 2,
        out_shape=[sds((members, rows, lanes), BF), sds((blocks, members, lanes), BF)],
        scratch_shapes=[pltpu.VMEM((members * (2 * cols + 8), lanes), F32),
                        pltpu.VMEM((blocks + 1, members, lanes), F32), dma],
        compiler_params=pltpu.CompilerParams(vmem_limit_bytes=8 * MIB),
        name="gather",
    )(start, away(control.reshape(members, rows, lanes)), e3, meta)

    n_bits = (n_lat.bit_length() - 1) + (n_lon.bit_length() - 1)
    p, px, e_ext, p_edge, upper = pl.pallas_call(
        functools.partial(exchange_kernel, dims, (n_lat, n_lon)),
        in_specs=[sm] + [vm] * 10,
        out_specs=[vm] * 5,
        out_shape=[sds((rows, lanes)), sds((2 * half, lanes)), sds((members, 2 * half, lanes), BF),
                   sds((groups, ext, lanes), BF), sds((members, members))],
        scratch_shapes=[
            pltpu.VMEM((blocks + 1, members, lanes), BF),
            pltpu.VMEM((blocks + 1, members, lanes), BF),
            pltpu.VMEM((2, 3, half, lanes), F32),
            pltpu.VMEM((2, 8, 2 * half), jnp.int32),
            pltpu.SMEM((2, 8, 2 * half), jnp.int32),
            pltpu.VMEM((groups, rows, lanes), BF),
            pltpu.VMEM((groups, rows, lanes), BF),
            pltpu.VMEM((2, groups, rows, lanes), BF),
            pltpu.VMEM((2, groups, rows, lanes), BF),
            pltpu.VMEM((2, groups, 2 * half, lanes), BF),
            pltpu.VMEM((groups, 2 * half, lanes), BF),
            pltpu.VMEM((members, 2 * half, lanes), BF),
            pltpu.VMEM((rows, lanes), F32),
            pltpu.VMEM((members * (2 * half + 8), lanes), F32),
            pltpu.VMEM((2, 2, half, lanes), F32),
            pltpu.VMEM((2, 2, half, lanes), F32),
            pltpu.VMEM((8, ext), F32),
            pltpu.VMEM((2, 8, ext), F32),
            pltpu.VMEM((n_bits, 2, members, lanes), F32),
            pltpu.VMEM((members, lanes), F32),
            pltpu.VMEM((2 * half, lanes), F32),
            dma((2, 3)), dma((2, 3)), dma((2, 2)), dma((2, 2)), dma((2, 1)), dma((2, 1)), dma((2,)), dma((2,)),
            dma((2, 1)), dma((2, 1)), dma((n_bits,)), dma((n_bits,)), dma,
        ],
        compiler_params=pltpu.CompilerParams(
            vmem_limit_bytes=16 * MIB, collective_id=0, has_side_effects=True),
        name="exchange",
    )(lat_taps, c3, e3, q, v, kf, lf, bf, packed, meta, start)

    block = 8 if members % 8 == 0 else 2
    gradient, upper = pl.pallas_call(
        functools.partial(adjoint_kernel, dims, block),
        grid=(members // block,),
        in_specs=[vm] * 10,
        out_specs=[pl.BlockSpec((block, rows, lanes), lambda g: (g, 0, 0)),
                   pl.BlockSpec((members, members), lambda g: (0, 0))],
        out_shape=[sds((members, rows, lanes)), sds((members, members))],
        scratch_shapes=[pltpu.VMEM((groups, rows, lanes), F32)],
        compiler_params=pltpu.CompilerParams(vmem_limit_bytes=8 * MIB),
        name="adjoint",
    )(c3, e3, e_ext, p, px, p_edge, ka, la, ba, upper)
    return gradient.reshape(members, levels, cols, lanes), upper


def solution(mesh):
    in_specs = (
        P(None, None, "lon", "lat"),
        P(None, None, "lon", "lat"),
        P(),
        P(),
        P(),
        P("lon", "lat", None),
        P("lon", "lat"),
        P("lon", "lat", None),
        P("lon", "lat", None),
        P("lon", "lat", None),
    )
    out_specs = (P(None, None, "lon", "lat"), P())
    return jax.shard_map(shards, mesh=mesh, in_specs=in_specs, out_specs=out_specs, check_vma=False)
```

```python
import functools

import jax
import jax.numpy as jnp
from jax import lax
from jax.experimental import pallas as pl
from jax.experimental.pallas import tpu as pltpu
from jax.sharding import PartitionSpec as P

OFFSETS = (-2, -1, 1, 2)
F32, BF = jnp.float32, jnp.bfloat16
MIB = 1024 * 1024
MESH = pl.DeviceIdType.MESH


def nn(a, b):
    return jnp.dot(a, b, preferred_element_type=F32)


def nt(a, b):
    return lax.dot_general(a, b, (((1,), (1,)), ((), ())), preferred_element_type=F32)


def tn(a, b):
    return lax.dot_general(a, b, (((0,), (0,)), ((), ())), preferred_element_type=F32)


def split(x):
    hi = x.astype(BF)
    return hi, (x - hi.astype(F32)).astype(BF)


def iota(shape, axis):
    return lax.broadcasted_iota(jnp.int32, shape, axis)


def band(diff, taps_ref, sign):
    out = jnp.where(diff == 0, 1.0, 0.0)
    for t, offset in enumerate(OFFSETS):
        out = out + jnp.where(diff == sign * offset, taps_ref[t], 0.0)
    return out


def halo_place(h, levels, cols):
    side = h // (2 * levels)
    rest = h - side * 2 * levels
    d = rest // levels
    return rest - d * levels, d + side * (cols - 2), d - 2 + side * (cols + 2)


def setup_kernel(dims, lat_hbm, lon_hbm, count_ref, e_hbm, mix_hbm, place_hbm, keep_hbm, weight_hbm, innov_hbm,
                 e_ref, kf_ref, ka_ref, lf_ref, la_ref, bf_ref, ba_ref, q_ref, v_ref, meta_ref, start_ref,
                 mix_ref, place_ref, keep_ref, weight_ref, innov_ref, lat_taps, lon_taps, sems):
    levels, cols, lanes = dims
    small = [pltpu.make_async_copy(a, b, sems.at[i]) for i, (a, b) in enumerate(
        ((mix_hbm, mix_ref), (place_hbm, place_ref), (keep_hbm, keep_ref), (weight_hbm, weight_ref),
         (innov_hbm, innov_ref), (lat_hbm, lat_taps), (lon_hbm, lon_taps)))]
    large = pltpu.make_async_copy(e_hbm, e_ref, sems.at[len(small)])
    for copy in small:
        copy.start()
    large.start()
    for copy in small:
        copy.wait()
    rows, half = levels * cols, 2 * levels
    ext = rows + 2 * half

    def ext_level_col(x):
        k, own, outer = halo_place(x - rows, levels, cols)
        inside = x < rows
        xk = x // cols
        return jnp.where(inside, xk, k), jnp.where(inside, x - xk * cols, own), jnp.where(
            inside, x - xk * cols, outer)

    diff = iota((lanes, lanes), 0) - iota((lanes, lanes), 1)
    lf_ref[...] = jnp.concatenate(split(band(diff, lat_taps, 1)), axis=0)
    la_ref[...] = jnp.concatenate(split(band(diff, lat_taps, -1)), axis=0)
    src, dst = iota((lanes, lanes), 0), iota((lanes, lanes), 1)
    member = (src // 4) == (dst // 4)
    t, u = src % 4, dst % 4
    at = jnp.where(t < 2, t - 2, lanes + t - 2) - jnp.where(u < 2, lanes - 2 + u, u - 2)
    bf_ref[...] = jnp.concatenate(split(jnp.where(member, band(at, lat_taps, 1), 0.0)), axis=0)
    ba_ref[...] = jnp.concatenate(split(jnp.where(member, band(at, lat_taps, -1), 0.0)), axis=0)
    mix = mix_ref[...]
    col = ext_level_col(iota((ext, 1), 0))[2]
    y = iota((1, rows), 1)
    taps = band((y - y // cols * cols) - col, lon_taps, 1)
    pick = (ext_level_col(iota((ext, 1), 0))[0] == iota((ext, levels), 1)).astype(F32).astype(BF)
    put = (iota((1, rows), 1) // cols == iota((levels, rows), 0)).astype(F32).astype(BF)
    hi, lo = split(nn(nn(pick, mix).astype(BF), put) * taps)
    kf_ref[:ext] = hi
    kf_ref[ext:] = lo
    col = ext_level_col(iota((1, ext), 1))[2]
    y = iota((rows, 1), 0)
    taps = band((y - y // cols * cols) - col, lon_taps, 1)
    pick = (ext_level_col(iota((1, ext), 1))[0] == iota((levels, ext), 0)).astype(F32).astype(BF)
    put = (iota((rows, 1), 0) // cols == iota((rows, levels), 1)).astype(F32).astype(BF)
    hi, lo = split(nn(put, nn(mix.T, pick).astype(BF)) * taps)
    ka_ref[:rows] = hi
    ka_ref[rows:] = lo
    slots = place_ref.shape[1]
    chunk = 512 if slots % 512 == 0 else slots
    ids_level, ids_col, _ = ext_level_col(iota((ext, 1), 0))
    ids = jnp.broadcast_to(ids_level * cols + ids_col, (ext, chunk))
    lane_ids = iota((lanes, chunk), 0)
    total = jnp.zeros((ext, 4 * lanes), F32)
    for s in range(0, slots, chunk):
        place = place_ref[:, s : s + chunk]
        r = place // lanes
        c = place - r * lanes
        live = (iota((1, chunk), 1) + s < count_ref[0, 0]).astype(F32) * keep_ref[:, s : s + chunk].astype(F32)
        q = live * weight_ref[:, s : s + chunk]
        v = q * innov_ref[:, s : s + chunk]
        hit = lane_ids == c
        parts = []
        for x in (q, v):
            for part in split(x):
                parts.append(jnp.where(hit, part.astype(F32), 0.0).astype(BF))
        total = total + nt((ids == r).astype(F32).astype(BF), jnp.concatenate(parts, axis=0))
    q = total[:, :lanes] + total[:, lanes : 2 * lanes]
    v = total[:, 2 * lanes : 3 * lanes] + total[:, 3 * lanes :]
    q_ref[...] = q[:rows]
    v_ref[...] = v[:rows]
    held = q[rows:] > 0.0
    occupied = held.astype(F32).astype(BF)
    n = 2 * half
    before = (iota((lanes, lanes), 0) < iota((lanes, lanes), 1)).astype(F32).astype(BF)
    above = (iota((n, n), 1) < iota((n, n), 0)).astype(F32).astype(BF)
    within = nn(occupied, before)
    start = nn(above, nn(occupied, jnp.ones((lanes, lanes), BF)).astype(BF))
    rank = (start + within).astype(jnp.int32)
    last = max(slots // lanes - 1, 0)
    block = jnp.minimum(start.astype(jnp.int32) // lanes, last)
    relative = jnp.where(held, rank - block * lanes, -1)
    count = nt(jnp.ones((8, lanes), BF), occupied).astype(BF)
    below = (iota((n, n), 0) < iota((n, n), 1)).astype(F32).astype(BF)
    start_ref[...] = jnp.minimum(nn(count, below).astype(jnp.int32) // lanes, last)
    for side in range(2):
        at = slice(side * half, (side + 1) * half)
        meta_ref[side, 0] = relative[at].astype(F32)
        meta_ref[side, 1] = q[rows:][at]
        meta_ref[side, 2] = v[rows:][at]
    large.wait()


def spot(relative_row, width):
    lanes = relative_row.shape[1]
    ranks = iota((width, lanes), 0).astype(F32)
    return jnp.where(jnp.broadcast_to(relative_row, (width, lanes)) == ranks, 1.0, 0.0).astype(BF)


def load_rows(ref, j, members, stride):
    return ref[pl.ds(j, members, stride=stride), :]


def gather_kernel(dims, start_ref, c_hbm, e_ref, meta_ref, c_ref, packed_ref, wide_ref, sum_ref, sem):
    levels, cols, lanes = dims
    members = e_ref.shape[0]
    half = 2 * levels
    per = 4
    pitch = per * cols + 8
    copy = pltpu.make_async_copy(c_hbm, c_ref, sem)
    copy.start()
    sum_ref[...] = jnp.zeros_like(sum_ref)

    def body(g, _):
        base = pl.multiple_of(g * per * cols, per * cols)
        x = e_ref[:, pl.ds(base, per * cols), :].astype(F32)
        for m in range(members):
            wide_ref[m * pitch : m * pitch + per * cols, :] = x[m]
        found = []
        for j in range(per * cols):
            col = j % cols
            if 2 <= col < cols - 2:
                continue
            side = int(col >= 2)
            h = (col - side * (cols - 2)) * levels + g * per + j // cols
            xb = load_rows(wide_ref, j, members, pitch).astype(BF)
            got = nt(xb, spot(meta_ref[side, 0, pl.ds(h, 1), :], 2 * lanes))
            found.append((start_ref[0, side * half + h], got))
        for b, got in found:
            sum_ref[b] += got[:, :lanes]
            sum_ref[b + 1] += got[:, lanes:]
        return 0

    lax.fori_loop(0, levels // per, body, 0)
    for b in range(packed_ref.shape[0]):
        packed_ref[b] = sum_ref[b].astype(BF)
    copy.wait()


def factor(s_ref, out_ref, size):
    lanes = s_ref.shape[1]
    step = 8
    lane = iota((step, lanes), 1)
    row = iota((step, lanes), 0)
    for b in range(0, size, step):
        panel = s_ref[b : b + step, :]
        cols = [jnp.broadcast_to(panel[:, b + i : b + i + 1], (step, lanes)) for i in range(step)]
        done = jnp.zeros((step, lanes), F32)
        for j in range(step):
            scale = lax.rsqrt(jnp.broadcast_to(cols[j][j : j + 1], (step, lanes)))
            across = jnp.broadcast_to(panel[j : j + 1], (step, lanes)) * scale
            done = jnp.where(row == j, across, done)
            down = cols[j] * scale
            panel = panel - down * across
            for i in range(j + 1, step):
                cols[i] = cols[i] - down * jnp.broadcast_to(down[i : i + 1], (step, lanes))
        done = jnp.where(lane >= b + row, done, 0.0)
        out_ref[b : b + step, :] = done[:, :size]
        if b + step < size:
            hi, lo = split(done)
            low = jnp.concatenate([hi, hi, lo], axis=0)
            high = jnp.concatenate([hi, lo, hi], axis=0)
            s_ref[...] = s_ref[...] - tn(low, high)[:size]


def stacked(a_ref, x, rows):
    piece = 128 if rows % 128 == 0 else rows
    parts = [nn(a_ref[r : r + piece], x) + nn(a_ref[rows + r : rows + r + piece], x) for r in range(0, rows, piece)]
    return jnp.concatenate(parts, axis=0) if len(parts) > 1 else parts[0]


def forward_loop(group, c_ref, e_ref, kf_ref, lf_ref, inc_ref, outer_ref, first, last):
    rows, lanes = inc_ref.shape
    ext = rows + outer_ref.shape[1]

    def body(step, _):
        for quad in range(0, group, 4):
            at = [group * step + quad + i for i in range(4)]
            smooth = []
            for m in at:
                x = c_ref[m]
                smooth.append(nn(jnp.concatenate([x, x], axis=1), lf_ref[...]).astype(BF))
            out = [stacked(kf_ref, jnp.concatenate(smooth[2 * i : 2 * i + 2], axis=1), ext) for i in range(2)]
            total = inc_ref[...]
            for i, m in enumerate(at):
                part = out[i // 2][:, i % 2 * lanes : (i % 2 + 1) * lanes]
                total = total + e_ref[m].astype(F32) * part[:rows]
                outer_ref[m] = part[rows:].astype(BF)
            inc_ref[...] = total
        return 0

    lax.fori_loop(first, last, body, 0)


def exchange_kernel(dims, sizes, c_ref, e_ref, q_ref, v_ref, kf_ref, lf_ref, bf_ref, packed_ref, meta_ref,
                    start_ref,
                    p_ref, px_ref, ext_ref, edge_ref, upper_ref,
                    got_left, got_right, got_meta, got_start, start_smem, own_c, own_e, lat_c, lat_e, lat_x, own_x, outer_ref,
                    inc_ref, wide_ref, send_inc, got_inc, p_edge, got_edge, gram_in, total_ref, given_ref,
                    far_sem, far_recv, lat_sem, lat_recv, x_sem, x_recv, inc_sem, inc_recv,
                    pe_sem, pe_recv, gram_sem, gram_recv, smem_sem):
    levels, cols, lanes = dims
    n_lat, n_lon = sizes
    members, rows = c_ref.shape[0], c_ref.shape[1]
    half = 2 * levels
    ext = rows + 2 * half
    per = lanes // 4
    groups = own_e.shape[0]
    lat, lon = lax.axis_index("lat"), lax.axis_index("lon")
    left, right = lax.rem(lon + n_lon - 1, n_lon), lax.rem(lon + 1, n_lon)
    has_before, has_after = lat > 0, lat < n_lat - 1

    def flip(x, bit):
        return x + bit - 2 * bit * (x // bit - x // (2 * bit) * 2)

    partners = [("lat", 1 << i) for i in range(n_lat.bit_length() - 1)]
    n_near = len(partners)
    partners += [("lon", 1 << i) for i in range(n_lon.bit_length() - 1)]
    barrier = pltpu.get_barrier_semaphore()

    def greet(where):
        pl.semaphore_signal(barrier, inc=1, device_id=where, device_id_type=MESH)

    greet({"lon": left})
    greet({"lon": right})

    @pl.when(has_before)
    def _():
        greet({"lat": lat - 1})

    @pl.when(has_after)
    def _():
        greet({"lat": lat + 1})

    for axis, bit in partners:
        greet({axis: flip(lat if axis == "lat" else lon, bit)})

    packed_at = iota((rows, lanes), 1) // 4
    for g in range(groups):
        first, last = g * per, min((g + 1) * per, members)
        for ref, own in ((c_ref, own_c), (e_ref, own_e)):
            def pack(k, x, first=first, ref=ref):
                for i in range(4):
                    m = first + 4 * k + i
                    x = jnp.where(packed_at == m - first, pltpu.roll(ref[m], 2 + 4 * (m - first), 1), x)
                return x

            own[g] = lax.fori_loop(0, (last - first) // 4, pack, jnp.zeros((rows, lanes), BF))

    pl.semaphore_wait(barrier, 2 + len(partners) + has_before.astype(jnp.int32) + has_after.astype(jnp.int32))

    def remote(src, dst, s, r, where):
        return pltpu.make_async_remote_copy(
            src_ref=src, dst_ref=dst, send_sem=s, recv_sem=r, device_id=where, device_id_type=MESH)

    blocks = packed_ref.shape[0]
    got = (got_left, got_right)
    far = []
    for slot, to in ((0, right), (1, left)):
        mine = 1 - slot
        far.append([
            remote(meta_ref.at[mine], got_meta.at[slot], far_sem.at[slot, 0], far_recv.at[slot, 0], {"lon": to}),
            remote(start_ref, got_start.at[slot], far_sem.at[slot, 1], far_recv.at[slot, 1], {"lon": to}),
            remote(packed_ref, got[slot].at[pl.ds(0, blocks)], far_sem.at[slot, 2], far_recv.at[slot, 2],
                   {"lon": to})])

    def lat_pair(src, dst, s, r, k):
        up = remote(src, dst.at[0], s.at[0, k], r.at[0, k], {"lat": lat + 1})
        down = remote(src, dst.at[1], s.at[1, k], r.at[1, k], {"lat": lat - 1})
        return up, down

    def lat_start(up, down):
        pl.when(has_after)(up.start)
        pl.when(has_before)(down.start)

    def lat_wait(up, down):
        pl.when(has_after)(up.wait_send)
        pl.when(has_before)(down.wait_send)
        pl.when(has_before)(up.wait_recv)
        pl.when(has_after)(down.wait_recv)

    near = [lat_pair(own_c, lat_c, lat_sem, lat_recv, 0), lat_pair(own_e, lat_e, lat_sem, lat_recv, 1)]
    for pair in near:
        lat_start(*pair)
    for copies in far:
        for copy in copies:
            copy.start()

    for side, missing in ((0, jnp.logical_not(has_before)), (1, jnp.logical_not(has_after))):
        @pl.when(missing)
        def _(side=side):
            for ref in (lat_c, lat_e, lat_x, got_edge):
                ref[side] = jnp.zeros_like(ref[side])

    for slot in range(2):
        got[slot][blocks] = jnp.zeros_like(got[slot][blocks])
    inc_ref[...] = jnp.zeros_like(inc_ref)

    two = 2
    pitch = two * cols + 8

    def grams(g, gram):
        gram = list(gram)
        base = pl.multiple_of(g * two * cols, two * cols)
        x = e_ref[:, pl.ds(base, two * cols), :].astype(F32)
        for m in range(members):
            wide_ref[m * pitch : m * pitch + two * cols, :] = x[m]
        weight = q_ref[pl.ds(base, two * cols), :]
        for pair in range(0, two * cols, 2):
            plain, his, los = [], [], []
            for j in (pair, pair + 1):
                y = load_rows(wide_ref, j, members, pitch)
                plain.append(y.astype(BF))
                hi, lo = split(y * weight[j : j + 1])
                his.append(hi)
                los.append(lo)
            weighted = jnp.concatenate([jnp.concatenate(his, axis=1), jnp.concatenate(los, axis=1)], axis=0)
            k = pair // 2 % 2
            gram[k] = gram[k] + nt(weighted, jnp.concatenate(plain, axis=1))
        return tuple(gram)

    zero = jnp.zeros((2 * members, members), F32)
    gram = lax.fori_loop(0, levels // two, grams, (zero, zero))
    gram = gram[0] + gram[1]
    total_ref[...] = jnp.zeros_like(total_ref)
    total_ref[:, :members] = gram[:members] + gram[members:]

    stages = []

    def stage_start():
        i = len(stages)
        if i < len(partners):
            axis, bit = partners[i]
            gram_in[i, 0] = total_ref[...]
            copy = remote(gram_in.at[i, 0], gram_in.at[i, 1], gram_sem.at[i], gram_recv.at[i],
                          {axis: flip(lat if axis == "lat" else lon, bit)})
            copy.start()
            stages.append(copy)

    def stage_end():
        i = len(stages) - 1
        stages[i].wait()
        total_ref[...] = total_ref[...] + gram_in[i, 1]

    group = 8 if members % 8 == 0 else 4
    cuts = [members // group * i // (n_near + 1) for i in range(n_near + 2)]
    for i in range(n_near + 1):
        stage_start()
        forward_loop(group, c_ref, e_ref, kf_ref, lf_ref, inc_ref, outer_ref, cuts[i], cuts[i + 1])
        if i < n_near:
            stage_end()

    for pair in near:
        lat_wait(*pair)
    before = iota((rows, lanes), 1) % 4 < 2
    spare = []
    for g in range(groups):
        halo = jnp.where(before, lat_c[0, g].astype(F32), lat_c[1, g].astype(F32)).astype(BF)
        mixed = nn(kf_ref[...], halo)
        mixed = (mixed[:ext] + mixed[ext:]).astype(BF)
        spare.append(nn(jnp.concatenate([mixed, mixed], axis=1), bf_ref[...]))
    source = iota((lanes, lanes), 0) % 4
    target = iota((lanes, lanes), 1)
    drop = (target == jnp.where(source < 2, lanes - 2 + source, source - 2)).astype(F32).astype(BF)

    def settle(products):
        total = None
        for x in products:
            part = nn(jnp.concatenate(split(x), axis=1), jnp.concatenate([drop, drop], axis=0))
            total = part if total is None else total + part
        return total

    inc_ref[...] += settle([own_e[g].astype(F32) * spare[g][:rows] for g in range(groups)])

    pitch_x = 2 * half + 8
    for slot in range(2):
        for copy in far[slot]:
            copy.wait()
        copy = pltpu.make_async_copy(got_start.at[slot], start_smem.at[slot], smem_sem)
        copy.start()
        copy.wait()

        def expand(k, _, slot=slot):
            for i in range(8):
                h = k * 8 + i
                b = start_smem[slot, 0, (1 - slot) * half + h]
                hot = spot(got_meta[slot, 0, pl.ds(h, 1), :], 2 * lanes)
                x = nn(jnp.concatenate([got[slot][b], got[slot][b + 1]], axis=1), hot)
                wide_ref[pl.ds(slot * half + h, members, stride=pitch_x), :] = x
            return 0

        lax.fori_loop(0, half // 8, expand, 0)
        if len(stages) > n_near:
            stage_end()
            stage_start()

    given_ref[...] = jnp.zeros_like(given_ref)
    for g in range(groups):
        first, last = g * per, min((g + 1) * per, members)

        def outer(k, carry, first=first):
            total, edges = carry
            for i in range(4):
                m = first + 4 * k + i
                x = wide_ref[pl.ds(pl.multiple_of(m * pitch_x, 8), 2 * half), :]
                xb = x.astype(BF)
                ext_ref[m] = xb
                total = total + x * outer_ref[m].astype(F32)
                edges = jnp.where(packed_at[: 2 * half] == m - first, pltpu.roll(xb, 2 + 4 * (m - first), 1), edges)
            return total, edges

        zero = jnp.zeros((2 * half, lanes), F32)
        total, edges = lax.fori_loop(0, (last - first) // 4, outer, (zero, zero.astype(BF)))
        given_ref[...] += total
        own_x[g] = edges
    given_ref[...] += settle([own_x[g].astype(F32) * spare[g][rows:] for g in range(groups)])

    for d in range(2):
        at = slice(d * levels, (d + 1) * levels)
        send_inc[0, 0, at] = inc_ref[pl.ds(cols - 2 + d, levels, stride=cols), :]
        send_inc[1, 0, at] = inc_ref[pl.ds(d, levels, stride=cols), :]
    send_inc[0, 1] = given_ref[half:]
    send_inc[1, 1] = given_ref[:half]
    swap = []
    for slot, to in ((0, right), (1, left)):
        swap.append(remote(send_inc.at[slot], got_inc.at[slot], inc_sem.at[slot], inc_recv.at[slot], {"lon": to}))
    for copy in swap:
        copy.start()
    across = lat_pair(own_x, lat_x, x_sem, x_recv, 0)
    lat_start(*across)

    while True:
        if stages:
            stage_end()
        if len(stages) == len(partners):
            break
        stage_start()
    eye = (iota((members, lanes), 0) == iota((members, lanes), 1)).astype(F32)
    total_obs = packed_ref.shape[0] * lanes * n_lat * n_lon
    total_ref[...] = eye + members / total_obs * total_ref[...]
    factor(total_ref, upper_ref, members)

    for copy in swap:
        copy.wait()
    for slot in range(2):
        px_ref[slot * half : (slot + 1) * half] = (
            got_meta[slot, 1] * (got_inc[slot, 0] + given_ref[slot * half : (slot + 1) * half]) - got_meta[slot, 2])
        for d in range(2):
            at = pl.ds(slot * (cols - 2) + d, levels, stride=cols)
            inc_ref[at, :] = inc_ref[at, :] + got_inc[slot, 1, d * levels : (d + 1) * levels]
    p_ref[...] = q_ref[...] * inc_ref[...] - v_ref[...]

    edge_row, edge_lane = iota((8, lanes), 0), iota((8, lanes), 1)
    pick = jnp.where(edge_lane == jnp.where(edge_row < 2, lanes - 2 + edge_row, edge_row - 2), 1.0, 0.0)
    pick = jnp.where(edge_row < 4, pick, 0.0).astype(BF)
    for ref, at in ((p_ref, slice(0, rows)), (px_ref, slice(rows, ext))):
        hi, lo = split(ref[...])
        p_edge[:, at] = nt(pick, hi) + nt(pick, lo)
    final = lat_pair(p_edge, got_edge, pe_sem, pe_recv, 0)
    lat_start(*final)
    lat_wait(*across)
    before = iota((ext, lanes), 1) % 4 < 2
    halo = []
    for g in range(groups):
        far_e = [jnp.concatenate([lat_e[side, g], lat_x[side, g]], axis=0).astype(F32) for side in range(2)]
        halo.append(jnp.where(before, far_e[0], far_e[1]))
    spread = jnp.where((edge_lane % 4 == edge_row) & (edge_row < 4), 1.0, 0.0).astype(BF)
    lat_wait(*final)
    p_halo = jnp.where(iota((8, ext), 0) < 2, got_edge[0], got_edge[1])
    hi, lo = split(p_halo)
    p_halo = tn(hi, spread) + tn(lo, spread)
    for g in range(groups):
        edge_ref[g] = (halo[g] * p_halo).astype(BF)


def adjoint_kernel(dims, block, c_ref, e_ref, ext_ref, p_ref, px_ref, pe_ref, ka_ref, la_ref, ba_ref, upper_ref,
                   out_ref, upper_out, edge_ref):
    levels, cols, lanes = dims
    members, rows = c_ref.shape[0], c_ref.shape[1]
    step = pl.program_id(0)
    per = lanes // 4

    @pl.when(step == 0)
    def _():
        upper_out[...] = upper_ref[...]
        for g in range(edge_ref.shape[0]):
            z = nn(ka_ref[...], pe_ref[g])
            z = (z[:rows] + z[rows:]).astype(BF)
            edge_ref[g] = nn(jnp.concatenate([z, z], axis=1), ba_ref[...])

    lane = iota((rows, lanes), 1)
    at_edge = (lane < 2) | (lane >= lanes - 2)
    p, px = p_ref[...], px_ref[...]

    for quad in range(block // 4):
        wide = []
        for i in range(4):
            m = step * block + 4 * quad + i
            own = (e_ref[m].astype(F32) * p).astype(BF)
            far = (ext_ref[m].astype(F32) * px).astype(BF)
            wide.append(jnp.concatenate([own, far], axis=0))
        mixed = [stacked(ka_ref, jnp.concatenate(wide[2 * i : 2 * i + 2], axis=1), rows).astype(BF) for i in range(2)]
        smooth = []
        for i in range(4):
            z = mixed[i // 2][:, i % 2 * lanes : (i % 2 + 1) * lanes]
            smooth.append(nn(jnp.concatenate([z, z], axis=1), la_ref[...]))
        for i in range(4):
            m = step * block + 4 * quad + i
            g = m // per
            turned = pltpu.roll(edge_ref[g], lax.rem(2 * lanes - 2 - 4 * (m - g * per), lanes), 1)
            out_ref[4 * quad + i] = c_ref[m].astype(F32) + smooth[i] + jnp.where(at_edge, turned, 0.0)


def shards(
    control, ensemble, level_mix, lat_taps, lon_taps, obs_location, obs_count, obs_keep, innovation, obs_weight
):
    members, levels, cols, lanes = control.shape
    dims = (levels, cols, lanes)
    rows, half = levels * cols, 2 * levels
    ext = rows + 2 * half
    slots = obs_location.shape[2]
    blocks = slots // lanes
    groups = -(-4 * members // lanes)
    n_lat, n_lon = lax.axis_size("lat"), lax.axis_size("lon")
    vm, sm = pl.BlockSpec(memory_space=pltpu.VMEM), pl.BlockSpec(memory_space=pltpu.SMEM)
    hbm = pl.BlockSpec(memory_space=pltpu.HBM)
    dma = pltpu.SemaphoreType.DMA
    away = functools.partial(pltpu.with_memory_space_constraint, memory_space=pltpu.HBM)

    def sds(shape, dtype=F32):
        return jax.ShapeDtypeStruct(shape, dtype)

    e3, kf, ka, lf, la, bf, ba, q, v, meta, start = pl.pallas_call(
        functools.partial(setup_kernel, dims),
        in_specs=[hbm, hbm, sm] + [hbm] * 6,
        out_specs=[vm] * 11,
        out_shape=[sds((members, rows, lanes), BF), sds((2 * ext, rows), BF), sds((2 * rows, ext), BF)]
        + [sds((2 * lanes, lanes), BF)] * 4
        + [sds((rows, lanes)), sds((rows, lanes)), sds((2, 3, half, lanes)), sds((8, 2 * half), jnp.int32)],
        scratch_shapes=[pltpu.VMEM((levels, levels), BF), pltpu.VMEM((1, slots), jnp.int32),
                        pltpu.VMEM((1, slots), jnp.int32), pltpu.VMEM((1, slots), F32), pltpu.VMEM((1, slots), F32),
                        pltpu.SMEM((4,), F32), pltpu.SMEM((4,), F32), dma((8,))],
        compiler_params=pltpu.CompilerParams(vmem_limit_bytes=8 * MIB),
        name="setup",
    )(away(lat_taps), away(lon_taps), obs_count, away(ensemble.reshape(members, rows, lanes)), away(level_mix),
      away(obs_location[0]), away(obs_keep[0]), away(obs_weight[0]), away(innovation[0]))

    c3, packed = pl.pallas_call(
        functools.partial(gather_kernel, dims),
        in_specs=[sm, hbm, vm, vm],
        out_specs=[vm] * 2,
        out_shape=[sds((members, rows, lanes), BF), sds((blocks, members, lanes), BF)],
        scratch_shapes=[pltpu.VMEM((members * (4 * cols + 8), lanes), F32),
                        pltpu.VMEM((blocks + 1, members, lanes), F32), dma],
        compiler_params=pltpu.CompilerParams(vmem_limit_bytes=8 * MIB),
        name="gather",
    )(start, away(control.reshape(members, rows, lanes)), e3, meta)

    n_bits = (n_lat.bit_length() - 1) + (n_lon.bit_length() - 1)
    p, px, e_ext, p_edge, upper = pl.pallas_call(
        functools.partial(exchange_kernel, dims, (n_lat, n_lon)),
        in_specs=[vm] * 10,
        out_specs=[vm] * 5,
        out_shape=[sds((rows, lanes)), sds((2 * half, lanes)), sds((members, 2 * half, lanes), BF),
                   sds((groups, ext, lanes), BF), sds((members, members))],
        scratch_shapes=[
            pltpu.VMEM((blocks + 1, members, lanes), BF),
            pltpu.VMEM((blocks + 1, members, lanes), BF),
            pltpu.VMEM((2, 3, half, lanes), F32),
            pltpu.VMEM((2, 8, 2 * half), jnp.int32),
            pltpu.SMEM((2, 8, 2 * half), jnp.int32),
            pltpu.VMEM((groups, rows, lanes), BF),
            pltpu.VMEM((groups, rows, lanes), BF),
            pltpu.VMEM((2, groups, rows, lanes), BF),
            pltpu.VMEM((2, groups, rows, lanes), BF),
            pltpu.VMEM((2, groups, 2 * half, lanes), BF),
            pltpu.VMEM((groups, 2 * half, lanes), BF),
            pltpu.VMEM((members, 2 * half, lanes), BF),
            pltpu.VMEM((rows, lanes), F32),
            pltpu.VMEM((members * (2 * half + 8), lanes), F32),
            pltpu.VMEM((2, 2, half, lanes), F32),
            pltpu.VMEM((2, 2, half, lanes), F32),
            pltpu.VMEM((8, ext), F32),
            pltpu.VMEM((2, 8, ext), F32),
            pltpu.VMEM((n_bits, 2, members, lanes), F32),
            pltpu.VMEM((members, lanes), F32),
            pltpu.VMEM((2 * half, lanes), F32),
            dma((2, 3)), dma((2, 3)), dma((2, 2)), dma((2, 2)), dma((2, 1)), dma((2, 1)), dma((2,)), dma((2,)),
            dma((2, 1)), dma((2, 1)), dma((n_bits,)), dma((n_bits,)), dma,
        ],
        compiler_params=pltpu.CompilerParams(
            vmem_limit_bytes=16 * MIB, collective_id=0, has_side_effects=True),
        name="exchange",
    )(c3, e3, q, v, kf, lf, bf, packed, meta, start)

    block = 8 if members % 8 == 0 else 4
    gradient, upper = pl.pallas_call(
        functools.partial(adjoint_kernel, dims, block),
        grid=(members // block,),
        in_specs=[vm] * 10,
        out_specs=[pl.BlockSpec((block, rows, lanes), lambda g: (g, 0, 0)),
                   pl.BlockSpec((members, members), lambda g: (0, 0))],
        out_shape=[sds((members, rows, lanes)), sds((members, members))],
        scratch_shapes=[pltpu.VMEM((groups, rows, lanes), F32)],
        compiler_params=pltpu.CompilerParams(vmem_limit_bytes=8 * MIB),
        name="adjoint",
    )(c3, e3, e_ext, p, px, p_edge, ka, la, ba, upper)
    return gradient.reshape(members, levels, cols, lanes), upper


def solution(mesh):
    in_specs = (
        P(None, None, "lon", "lat"),
        P(None, None, "lon", "lat"),
        P(),
        P(),
        P(),
        P("lon", "lat", None),
        P("lon", "lat"),
        P("lon", "lat", None),
        P("lon", "lat", None),
        P("lon", "lat", None),
    )
    out_specs = (P(None, None, "lon", "lat"), P())
    return jax.shard_map(shards, mesh=mesh, in_specs=in_specs, out_specs=out_specs, check_vma=False)
```

```python
import functools

import jax
import jax.numpy as jnp
from jax import lax
from jax.experimental import pallas as pl
from jax.experimental.pallas import tpu as pltpu
from jax.sharding import PartitionSpec as P

OFFSETS = (-2, -1, 1, 2)
F32, BF = jnp.float32, jnp.bfloat16
MIB = 1024 * 1024
BLOCK = 16
MESH = pl.DeviceIdType.MESH


def nn(a, b):
    return jnp.dot(a, b, preferred_element_type=F32)


def nt(a, b):
    return lax.dot_general(a, b, (((1,), (1,)), ((), ())), preferred_element_type=F32)


def tn(a, b):
    return lax.dot_general(a, b, (((0,), (0,)), ((), ())), preferred_element_type=F32)


def split(x):
    hi = x.astype(BF)
    return hi, (x - hi.astype(F32)).astype(BF)


def iota(shape, axis):
    return lax.broadcasted_iota(jnp.int32, shape, axis)


def band(diff, taps_ref, sign):
    out = jnp.where(diff == 0, 1.0, 0.0)
    for t, offset in enumerate(OFFSETS):
        out = out + jnp.where(diff == sign * offset, taps_ref[t], 0.0)
    return out


def halo_place(h, levels, cols):
    side = h // (2 * levels)
    rest = h - side * 2 * levels
    d = rest // levels
    return rest - d * levels, d + side * (cols - 2), d - 2 + side * (cols + 2)


def setup_kernel(dims, lat_hbm, lon_hbm, count_ref, e_hbm, mix_hbm, place_hbm, keep_hbm, weight_hbm, innov_hbm,
                 e_ref, kf_ref, ka_ref, lf_ref, la_ref, bf_ref, ba_ref, q_ref, v_ref, meta_ref, start_ref,
                 mix_ref, place_ref, keep_ref, weight_ref, innov_ref, lat_taps, lon_taps, sems):
    levels, cols, lanes = dims
    small = [pltpu.make_async_copy(a, b, sems.at[i]) for i, (a, b) in enumerate(
        ((mix_hbm, mix_ref), (place_hbm, place_ref), (keep_hbm, keep_ref), (weight_hbm, weight_ref),
         (innov_hbm, innov_ref), (lat_hbm, lat_taps), (lon_hbm, lon_taps)))]
    large = pltpu.make_async_copy(e_hbm, e_ref, sems.at[len(small)])
    for copy in small:
        copy.start()
    large.start()
    for copy in small:
        copy.wait()
    rows, half = levels * cols, 2 * levels
    ext = rows + 2 * half

    def ext_level_col(x):
        k, own, outer = halo_place(x - rows, levels, cols)
        inside = x < rows
        xk = x // cols
        return jnp.where(inside, xk, k), jnp.where(inside, x - xk * cols, own), jnp.where(
            inside, x - xk * cols, outer)

    diff = iota((lanes, lanes), 0) - iota((lanes, lanes), 1)
    lf_ref[...] = jnp.concatenate(split(band(diff, lat_taps, 1)), axis=0)
    la_ref[...] = jnp.concatenate(split(band(diff, lat_taps, -1)), axis=0)
    src, dst = iota((lanes, lanes), 0), iota((lanes, lanes), 1)
    member = (src // 4) == (dst // 4)
    t, u = src % 4, dst % 4
    at = jnp.where(t < 2, t - 2, lanes + t - 2) - jnp.where(u < 2, lanes - 2 + u, u - 2)
    bf_ref[...] = jnp.concatenate(split(jnp.where(member, band(at, lat_taps, 1), 0.0)), axis=0)
    ba_ref[...] = jnp.concatenate(split(jnp.where(member, band(at, lat_taps, -1), 0.0)), axis=0)
    mix = mix_ref[...]
    col = ext_level_col(iota((ext, 1), 0))[2]
    y = iota((1, rows), 1)
    taps = band((y - y // cols * cols) - col, lon_taps, 1)
    pick = (ext_level_col(iota((ext, 1), 0))[0] == iota((ext, levels), 1)).astype(F32).astype(BF)
    put = (iota((1, rows), 1) // cols == iota((levels, rows), 0)).astype(F32).astype(BF)
    kf_ref[...] = (nn(nn(pick, mix).astype(BF), put) * taps).astype(BF)
    col = ext_level_col(iota((1, ext), 1))[2]
    y = iota((rows, 1), 0)
    taps = band((y - y // cols * cols) - col, lon_taps, 1)
    pick = (ext_level_col(iota((1, ext), 1))[0] == iota((levels, ext), 0)).astype(F32).astype(BF)
    put = (iota((rows, 1), 0) // cols == iota((rows, levels), 1)).astype(F32).astype(BF)
    ka_ref[...] = (nn(put, nn(mix.T, pick).astype(BF)) * taps).astype(BF)
    slots = place_ref.shape[1]
    chunk = 512 if slots % 512 == 0 else slots
    ids_level, ids_col, _ = ext_level_col(iota((ext, 1), 0))
    ids = jnp.broadcast_to(ids_level * cols + ids_col, (ext, chunk))
    lane_ids = iota((lanes, chunk), 0)
    total = jnp.zeros((ext, 4 * lanes), F32)
    for s in range(0, slots, chunk):
        place = place_ref[:, s : s + chunk]
        r = place // lanes
        c = place - r * lanes
        live = (iota((1, chunk), 1) + s < count_ref[0, 0]).astype(F32) * keep_ref[:, s : s + chunk].astype(F32)
        q = live * weight_ref[:, s : s + chunk]
        v = q * innov_ref[:, s : s + chunk]
        hit = lane_ids == c
        parts = []
        for x in (q, v):
            for part in split(x):
                parts.append(jnp.where(hit, part.astype(F32), 0.0).astype(BF))
        total = total + nt((ids == r).astype(F32).astype(BF), jnp.concatenate(parts, axis=0))
    q = total[:, :lanes] + total[:, lanes : 2 * lanes]
    v = total[:, 2 * lanes : 3 * lanes] + total[:, 3 * lanes :]
    q_ref[...] = q[:rows]
    v_ref[...] = v[:rows]
    held = q[rows:] > 0.0
    occupied = held.astype(F32).astype(BF)
    n = 2 * half
    before = (iota((lanes, lanes), 0) < iota((lanes, lanes), 1)).astype(F32).astype(BF)
    within = nn(occupied, before)
    relative = jnp.where(held, within, -2.0 * lanes)
    count = nt(jnp.ones((8, lanes), BF), occupied).astype(BF)
    below = (iota((n, n), 0) < iota((n, n), 1)).astype(F32).astype(BF)
    start_ref[...] = nn(count, below).astype(jnp.int32)
    for side in range(2):
        at = slice(side * half, (side + 1) * half)
        meta_ref[side, 0] = relative[at]
        meta_ref[side, 1] = q[rows:][at]
        meta_ref[side, 2] = v[rows:][at]
    large.wait()


def spot(relative_row, width):
    lanes = relative_row.shape[1]
    ranks = iota((width, lanes), 0).astype(F32)
    return jnp.where(jnp.broadcast_to(relative_row, (width, lanes)) == ranks, 1.0, 0.0).astype(BF)


def load_rows(ref, j, members, stride):
    return ref[pl.ds(j, members, stride=stride), :]


def gather_kernel(dims, start_ref, c_hbm, e_ref, meta_ref, c_ref, packed_ref, wide_ref, *rest):
    levels, cols, lanes = dims
    members = e_ref.shape[0]
    half = 2 * levels
    per = 4
    pitch = per * cols + 8
    sums, sem = rest[:4], rest[4]
    copy = pltpu.make_async_copy(c_hbm, c_ref, sem)
    copy.start()
    for ref in sums:
        ref[...] = jnp.zeros_like(ref)
    lane = iota((members, lanes), 1)

    def body(g, _):
        base = pl.multiple_of(g * per * cols, per * cols)
        x = e_ref[:, pl.ds(base, per * cols), :].astype(F32)
        for m in range(members):
            wide_ref[m * pitch : m * pitch + per * cols, :] = x[m]
        found = []
        for j in range(per * cols):
            col = j % cols
            if 2 <= col < cols - 2:
                continue
            side = int(col >= 2)
            h = (col - side * (cols - 2)) * levels + g * per + j // cols
            xb = load_rows(wide_ref, j, members, pitch).astype(BF)
            got = nt(xb, spot(meta_ref[side, 0, pl.ds(h, 1), :], lanes))
            first = start_ref[0, side * half + h]
            b = first // lanes
            found.append((sums[2 * side + col - side * (cols - 2)], b, first - b * lanes, got))
        for sum_ref, b, shift, got in found:
            got = pltpu.roll(got, shift, 1)
            sum_ref[b] += jnp.where(lane >= shift, got, 0.0)
            sum_ref[b + 1] += jnp.where(lane < shift, got, 0.0)
        return 0

    lax.fori_loop(0, levels // per, body, 0)
    for b in range(packed_ref.shape[0]):
        packed_ref[b] = ((sums[0][b] + sums[1][b]) + (sums[2][b] + sums[3][b])).astype(BF)
    copy.wait()


def factor(s_ref, out_ref, size):
    lanes = s_ref.shape[1]
    step = 8
    lane = iota((step, lanes), 1)
    row = iota((step, lanes), 0)
    for b in range(0, size, step):
        panel = s_ref[b : b + step, :]
        cols = [jnp.broadcast_to(panel[:, b + i : b + i + 1], (step, lanes)) for i in range(step)]
        done = jnp.zeros((step, lanes), F32)
        for j in range(step):
            scale = lax.rsqrt(jnp.broadcast_to(cols[j][j : j + 1], (step, lanes)))
            across = jnp.broadcast_to(panel[j : j + 1], (step, lanes)) * scale
            done = jnp.where(row == j, across, done)
            down = cols[j] * scale
            panel = panel - down * across
            for i in range(j + 1, step):
                cols[i] = cols[i] - down * jnp.broadcast_to(down[i : i + 1], (step, lanes))
        done = jnp.where(lane >= b + row, done, 0.0)
        out_ref[b : b + step, :] = done[:, :size]
        if b + step < size:
            hi, lo = split(done)
            low = jnp.concatenate([hi, hi, lo], axis=0)
            high = jnp.concatenate([hi, lo, hi], axis=0)
            s_ref[...] = s_ref[...] - tn(low, high)[:size]


def forward_loop(group, c_ref, e_ref, kf_ref, lf_ref, inc_ref, outer_ref, first, last):
    rows, lanes = inc_ref.shape
    ext = rows + outer_ref.shape[1]

    def body(step, _):
        for quad in range(0, group, 4):
            at = [group * step + quad + i for i in range(4)]
            smooth = []
            for m in at:
                x = c_ref[m]
                smooth.append(nn(jnp.concatenate([x, x], axis=1), lf_ref[...]).astype(BF))
            out = [nn(kf_ref[...], jnp.concatenate(smooth[2 * i : 2 * i + 2], axis=1)) for i in range(2)]
            total = inc_ref[...]
            for i, m in enumerate(at):
                part = out[i // 2][:, i % 2 * lanes : (i % 2 + 1) * lanes]
                total = total + e_ref[m].astype(F32) * part[:rows]
                outer_ref[m] = part[rows:].astype(BF)
            inc_ref[...] = total
        return 0

    lax.fori_loop(first, last, body, 0)


def exchange_kernel(dims, sizes, c_ref, e_ref, q_ref, v_ref, kf_ref, lf_ref, bf_ref, packed_ref, meta_ref,
                    start_ref,
                    p_ref, px_ref, ext_ref, edge_ref, upper_ref,
                    got_left, got_right, got_meta, got_start, start_smem, own_c, own_e, lat_c, lat_e, lat_x, own_x, outer_ref,
                    inc_ref, wide_ref, send_part, got_part, send_give, got_give, p_edge, got_edge, gram_in, total_ref,
                    far_sem, far_recv, lat_sem, lat_recv, x_sem, x_recv, inc_sem, inc_recv, give_sem, give_recv,
                    pe_sem, pe_recv, gram_sem, gram_recv, smem_sem):
    levels, cols, lanes = dims
    n_lat, n_lon = sizes
    members, rows = c_ref.shape[0], c_ref.shape[1]
    half = 2 * levels
    ext = rows + 2 * half
    per = lanes // 4
    groups = own_e.shape[0]
    lat, lon = lax.axis_index("lat"), lax.axis_index("lon")
    left, right = lax.rem(lon + n_lon - 1, n_lon), lax.rem(lon + 1, n_lon)
    has_before, has_after = lat > 0, lat < n_lat - 1

    def flip(x, bit):
        return x + bit - 2 * bit * (x // bit - x // (2 * bit) * 2)

    partners = [("lat", 1 << i) for i in range(n_lat.bit_length() - 1)]
    n_near = len(partners)
    partners += [("lon", 1 << i) for i in range(n_lon.bit_length() - 1)]
    barrier = pltpu.get_barrier_semaphore()

    def greet(where):
        pl.semaphore_signal(barrier, inc=1, device_id=where, device_id_type=MESH)

    greet({"lon": left})
    greet({"lon": right})

    @pl.when(has_before)
    def _():
        greet({"lat": lat - 1})

    @pl.when(has_after)
    def _():
        greet({"lat": lat + 1})

    for axis, bit in partners:
        greet({axis: flip(lat if axis == "lat" else lon, bit)})

    packed_at = iota((rows, lanes), 1) // 4

    def pack_edges(ref, own):
        for g in range(groups):
            first, last = g * per, min((g + 1) * per, members)

            def pack(k, x, first=first):
                for i in range(4):
                    m = first + 4 * k + i
                    x = jnp.where(packed_at == m - first, pltpu.roll(ref[m], 2 + 4 * (m - first), 1), x)
                return x

            own[g] = lax.fori_loop(0, (last - first) // 4, pack, jnp.zeros((rows, lanes), BF))

    pack_edges(c_ref, own_c)
    pl.semaphore_wait(barrier, 2 + len(partners) + has_before.astype(jnp.int32) + has_after.astype(jnp.int32))

    def remote(src, dst, s, r, where):
        return pltpu.make_async_remote_copy(
            src_ref=src, dst_ref=dst, send_sem=s, recv_sem=r, device_id=where, device_id_type=MESH)

    blocks = packed_ref.shape[0]
    got = (got_left, got_right)
    far = []
    for slot, to in ((0, right), (1, left)):
        mine = 1 - slot
        far.append([
            remote(meta_ref.at[mine], got_meta.at[slot], far_sem.at[slot, 0], far_recv.at[slot, 0], {"lon": to}),
            remote(start_ref, got_start.at[slot], far_sem.at[slot, 1], far_recv.at[slot, 1], {"lon": to}),
            remote(packed_ref, got[slot].at[pl.ds(0, blocks)], far_sem.at[slot, 2], far_recv.at[slot, 2],
                   {"lon": to})])

    def lat_pair(src, dst, s, r, k):
        up = remote(src, dst.at[0], s.at[0, k], r.at[0, k], {"lat": lat + 1})
        down = remote(src, dst.at[1], s.at[1, k], r.at[1, k], {"lat": lat - 1})
        return up, down

    def lat_start(up, down):
        pl.when(has_after)(up.start)
        pl.when(has_before)(down.start)

    def lat_wait(up, down):
        pl.when(has_after)(up.wait_send)
        pl.when(has_before)(down.wait_send)
        pl.when(has_before)(up.wait_recv)
        pl.when(has_after)(down.wait_recv)

    for copies in far:
        for copy in copies[:2]:
            copy.start()
    for copies in far:
        copies[2].start()
    near = lat_pair(own_c, lat_c, lat_sem, lat_recv, 0)
    lat_start(*near)
    pack_edges(e_ref, own_e)

    for side, missing in ((0, jnp.logical_not(has_before)), (1, jnp.logical_not(has_after))):
        @pl.when(missing)
        def _(side=side):
            for ref in (lat_c, lat_e, lat_x, got_edge):
                ref[side] = jnp.zeros_like(ref[side])

    for slot in range(2):
        got[slot][blocks:] = jnp.zeros_like(got[slot][blocks:])
    inc_ref[...] = jnp.zeros_like(inc_ref)

    two = 2
    pitch = two * cols + 8

    def grams(g, gram):
        gram = list(gram)
        base = pl.multiple_of(g * two * cols, two * cols)
        x = e_ref[:, pl.ds(base, two * cols), :].astype(F32)
        for m in range(members):
            wide_ref[m * pitch : m * pitch + two * cols, :] = x[m]
        weight = q_ref[pl.ds(base, two * cols), :]
        for pair in range(0, two * cols, 2):
            plain, his, los = [], [], []
            for j in (pair, pair + 1):
                y = load_rows(wide_ref, j, members, pitch)
                plain.append(y.astype(BF))
                hi, lo = split(y * weight[j : j + 1])
                his.append(hi)
                los.append(lo)
            weighted = jnp.concatenate([jnp.concatenate(his, axis=1), jnp.concatenate(los, axis=1)], axis=0)
            k = pair // 2 % 2
            gram[k] = gram[k] + nt(weighted, jnp.concatenate(plain, axis=1))
        return tuple(gram)

    zero = jnp.zeros((2 * members, members), F32)
    gram = lax.fori_loop(0, levels // two, grams, (zero, zero))
    gram = gram[0] + gram[1]
    total_ref[...] = jnp.zeros_like(total_ref)
    total_ref[:, :members] = gram[:members] + gram[members:]

    stages, ended = [], []

    def stage_start():
        i = len(stages)
        if i < len(partners):
            axis, bit = partners[i]
            gram_in[i, 0] = total_ref[...]
            copy = remote(gram_in.at[i, 0], gram_in.at[i, 1], gram_sem.at[i], gram_recv.at[i],
                          {axis: flip(lat if axis == "lat" else lon, bit)})
            copy.start()
            stages.append(copy)

    def stage_end():
        if len(ended) < len(stages):
            i = len(ended)
            stages[i].wait()
            total_ref[...] = total_ref[...] + gram_in[i, 1]
            ended.append(i)

    group = 8 if members % 8 == 0 else 4
    turns = members // group
    cuts = [min(2 * i, turns) for i in range(n_near + 1)] + [turns]
    for i in range(n_near + 1):
        stage_start()
        forward_loop(group, c_ref, e_ref, kf_ref, lf_ref, inc_ref, outer_ref, cuts[i], cuts[i + 1])
        if i < n_near:
            stage_end()

    lat_wait(*near)
    near_e = lat_pair(own_e, lat_e, lat_sem, lat_recv, 1)
    lat_start(*near_e)
    before = iota((rows, lanes), 1) % 4 < 2
    spare = []
    for g in range(groups):
        halo = jnp.where(before, lat_c[0, g].astype(F32), lat_c[1, g].astype(F32)).astype(BF)
        mixed = nn(kf_ref[...], halo).astype(BF)
        spare.append(nn(jnp.concatenate([mixed, mixed], axis=1), bf_ref[...]))
    source = iota((lanes, lanes), 0) % 4
    target = iota((lanes, lanes), 1)
    drop = (target == jnp.where(source < 2, lanes - 2 + source, source - 2)).astype(F32).astype(BF)

    def settle(products):
        total = None
        for x in products:
            part = nn(jnp.concatenate(split(x), axis=1), jnp.concatenate([drop, drop], axis=0))
            total = part if total is None else total + part
        return total

    inc_ref[...] += settle([own_e[g].astype(F32) * spare[g][:rows] for g in range(groups)])

    for d in range(2):
        at = slice(d * levels, (d + 1) * levels)
        send_part[0, at] = inc_ref[pl.ds(cols - 2 + d, levels, stride=cols), :]
        send_part[1, at] = inc_ref[pl.ds(d, levels, stride=cols), :]
    swap = []
    for slot, to in ((0, right), (1, left)):
        swap.append(remote(send_part.at[slot], got_part.at[slot], inc_sem.at[slot], inc_recv.at[slot], {"lon": to}))
        swap[-1].start()

    local = []
    for slot in range(2):
        for copy in far[slot][:2]:
            copy.wait()
        local.append(pltpu.make_async_copy(got_start.at[slot], start_smem.at[slot], smem_sem.at[slot]))
        local[-1].start()
    for copy in local:
        copy.wait()
    pitch_x = half + 8
    for slot in range(2):
        far[slot][2].wait()

        def expand(k, _, slot=slot):
            for i in range(8):
                h = k * 8 + i
                start = start_smem[slot, 0, (1 - slot) * half + h]
                b = start // lanes
                shift = (start - b * lanes).astype(F32)
                hot = spot(got_meta[slot, 0, pl.ds(h, 1), :] + shift, 2 * lanes)
                x = nn(jnp.concatenate([got[slot][b], got[slot][b + 1]], axis=1), hot)
                wide_ref[pl.ds(h, members, stride=pitch_x), :] = x
            return 0

        lax.fori_loop(0, half // 8, expand, 0)
        if len(stages) > n_near:
            stage_end()
            stage_start()
        at_x = slice(slot * half, (slot + 1) * half)
        given = jnp.zeros((half, lanes), F32)
        for g in range(groups):
            first, last = g * per, min((g + 1) * per, members)

            def outer(k, carry, first=first, at_x=at_x):
                total, edges = carry
                for i in range(group):
                    m = first + group * k + i
                    x = wide_ref[pl.ds(pl.multiple_of(m * pitch_x, 8), half), :]
                    xb = x.astype(BF)
                    ext_ref[m, at_x] = xb
                    total = total + x * outer_ref[m, at_x].astype(F32)
                    edges = jnp.where(packed_at[:half] == m - first, pltpu.roll(xb, 2 + 4 * (m - first), 1), edges)
                return total, edges

            given, edges = lax.fori_loop(0, (last - first) // group, outer, (given, jnp.zeros((half, lanes), BF)))
            own_x[g, at_x] = edges
        from_row = rows + slot * half
        send_give[slot] = given + settle(
            [own_x[g, at_x].astype(F32) * spare[g][from_row : from_row + half] for g in range(groups)])
        swap.append(remote(send_give.at[slot], got_give.at[1 - slot], give_sem.at[slot], give_recv.at[1 - slot],
                           {"lon": (left, right)[slot]}))
        swap[-1].start()
    across = lat_pair(own_x, lat_x, x_sem, x_recv, 0)
    lat_start(*across)

    while len(ended) < len(partners):
        stage_end()
        stage_start()
    eye = (iota((members, lanes), 0) == iota((members, lanes), 1)).astype(F32)
    total_obs = packed_ref.shape[0] * lanes * n_lat * n_lon
    total_ref[...] = eye + members / total_obs * total_ref[...]
    factor(total_ref, upper_ref, members)

    for copy in swap:
        copy.wait()
    for slot in range(2):
        px_ref[slot * half : (slot + 1) * half] = (
            got_meta[slot, 1] * (got_part[slot] + send_give[slot]) - got_meta[slot, 2])
        for d in range(2):
            at = pl.ds(slot * (cols - 2) + d, levels, stride=cols)
            inc_ref[at, :] = inc_ref[at, :] + got_give[slot, d * levels : (d + 1) * levels]
    p_ref[...] = q_ref[...] * inc_ref[...] - v_ref[...]

    edge_row, edge_lane = iota((8, lanes), 0), iota((8, lanes), 1)
    pick = jnp.where(edge_lane == jnp.where(edge_row < 2, lanes - 2 + edge_row, edge_row - 2), 1.0, 0.0)
    pick = jnp.where(edge_row < 4, pick, 0.0).astype(BF)
    for ref, at in ((p_ref, slice(0, rows)), (px_ref, slice(rows, ext))):
        hi, lo = split(ref[...])
        p_edge[:, at] = nt(pick, hi) + nt(pick, lo)
    lat_wait(*near_e)
    final = lat_pair(p_edge, got_edge, pe_sem, pe_recv, 0)
    lat_start(*final)
    lat_wait(*across)
    before = iota((ext, lanes), 1) % 4 < 2
    halo = []
    for g in range(groups):
        far_e = [jnp.concatenate([lat_e[side, g], lat_x[side, g]], axis=0).astype(F32) for side in range(2)]
        halo.append(jnp.where(before, far_e[0], far_e[1]))
    spread = jnp.where((edge_lane % 4 == edge_row) & (edge_row < 4), 1.0, 0.0).astype(BF)
    lat_wait(*final)
    p_halo = jnp.where(iota((8, ext), 0) < 2, got_edge[0], got_edge[1])
    hi, lo = split(p_halo)
    p_halo = tn(hi, spread) + tn(lo, spread)
    for g in range(groups):
        edge_ref[g] = (halo[g] * p_halo).astype(BF)


def adjoint_kernel(dims, block, c_ref, e_ref, ext_ref, p_ref, px_ref, pe_ref, ka_ref, la_ref, ba_ref, upper_ref,
                   out_ref, upper_out, edge_ref):
    levels, cols, lanes = dims
    members, rows = c_ref.shape[0], c_ref.shape[1]
    step = pl.program_id(0)
    per = lanes // 4

    @pl.when(step == 0)
    def _():
        upper_out[...] = upper_ref[...]
        for g in range(edge_ref.shape[0]):
            z = nn(ka_ref[...], pe_ref[g]).astype(BF)
            edge_ref[g] = nn(jnp.concatenate([z, z], axis=1), ba_ref[...])

    lane = iota((rows, lanes), 1)
    at_edge = (lane < 2) | (lane >= lanes - 2)
    p, px = p_ref[...], px_ref[...]

    for quad in range(block // 4):
        wide = []
        for i in range(4):
            m = step * block + 4 * quad + i
            own = (e_ref[m].astype(F32) * p).astype(BF)
            far = (ext_ref[m].astype(F32) * px).astype(BF)
            wide.append(jnp.concatenate([own, far], axis=0))
        mixed = [nn(ka_ref[...], jnp.concatenate(wide[2 * i : 2 * i + 2], axis=1)).astype(BF) for i in range(2)]
        smooth = []
        for i in range(4):
            z = mixed[i // 2][:, i % 2 * lanes : (i % 2 + 1) * lanes]
            smooth.append(nn(jnp.concatenate([z, z], axis=1), la_ref[...]))
        for i in range(4):
            m = step * block + 4 * quad + i
            g = m // per
            turned = pltpu.roll(edge_ref[g], lax.rem(2 * lanes - 2 - 4 * (m - g * per), lanes), 1)
            out_ref[4 * quad + i] = c_ref[m].astype(F32) + smooth[i] + jnp.where(at_edge, turned, 0.0)


def shards(
    control, ensemble, level_mix, lat_taps, lon_taps, obs_location, obs_count, obs_keep, innovation, obs_weight
):
    members, levels, cols, lanes = control.shape
    dims = (levels, cols, lanes)
    rows, half = levels * cols, 2 * levels
    ext = rows + 2 * half
    slots = obs_location.shape[2]
    blocks = slots // lanes
    groups = -(-4 * members // lanes)
    n_lat, n_lon = lax.axis_size("lat"), lax.axis_size("lon")
    vm, sm = pl.BlockSpec(memory_space=pltpu.VMEM), pl.BlockSpec(memory_space=pltpu.SMEM)
    hbm = pl.BlockSpec(memory_space=pltpu.HBM)
    dma = pltpu.SemaphoreType.DMA
    away = functools.partial(pltpu.with_memory_space_constraint, memory_space=pltpu.HBM)

    def sds(shape, dtype=F32):
        return jax.ShapeDtypeStruct(shape, dtype)

    e3, kf, ka, lf, la, bf, ba, q, v, meta, start = pl.pallas_call(
        functools.partial(setup_kernel, dims),
        in_specs=[hbm, hbm, sm] + [hbm] * 6,
        out_specs=[vm] * 11,
        out_shape=[sds((members, rows, lanes), BF), sds((ext, rows), BF), sds((rows, ext), BF)]
        + [sds((2 * lanes, lanes), BF)] * 4
        + [sds((rows, lanes)), sds((rows, lanes)), sds((2, 3, half, lanes)), sds((8, 2 * half), jnp.int32)],
        scratch_shapes=[pltpu.VMEM((levels, levels), BF), pltpu.VMEM((1, slots), jnp.int32),
                        pltpu.VMEM((1, slots), jnp.int32), pltpu.VMEM((1, slots), F32), pltpu.VMEM((1, slots), F32),
                        pltpu.SMEM((4,), F32), pltpu.SMEM((4,), F32), dma((8,))],
        compiler_params=pltpu.CompilerParams(vmem_limit_bytes=8 * MIB),
        name="setup",
    )(away(lat_taps), away(lon_taps), obs_count, away(ensemble.reshape(members, rows, lanes)), away(level_mix),
      away(obs_location[0]), away(obs_keep[0]), away(obs_weight[0]), away(innovation[0]))

    c3, packed = pl.pallas_call(
        functools.partial(gather_kernel, dims),
        in_specs=[sm, hbm, vm, vm],
        out_specs=[vm] * 2,
        out_shape=[sds((members, rows, lanes), BF), sds((blocks, members, lanes), BF)],
        scratch_shapes=[pltpu.VMEM((members * (4 * cols + 8), lanes), F32),
                        *[pltpu.VMEM((blocks + 2, members, lanes), F32)] * 4, dma],
        compiler_params=pltpu.CompilerParams(vmem_limit_bytes=8 * MIB),
        name="gather",
    )(start, away(control.reshape(members, rows, lanes)), e3, meta)

    n_bits = (n_lat.bit_length() - 1) + (n_lon.bit_length() - 1)
    p, px, e_ext, p_edge, upper = pl.pallas_call(
        functools.partial(exchange_kernel, dims, (n_lat, n_lon)),
        in_specs=[vm] * 10,
        out_specs=[vm] * 5,
        out_shape=[sds((rows, lanes)), sds((2 * half, lanes)), sds((members, 2 * half, lanes), BF),
                   sds((groups, ext, lanes), BF), sds((members, members))],
        scratch_shapes=[
            pltpu.VMEM((blocks + 2, members, lanes), BF),
            pltpu.VMEM((blocks + 2, members, lanes), BF),
            pltpu.VMEM((2, 3, half, lanes), F32),
            pltpu.VMEM((2, 8, 2 * half), jnp.int32),
            pltpu.SMEM((2, 8, 2 * half), jnp.int32),
            pltpu.VMEM((groups, rows, lanes), BF),
            pltpu.VMEM((groups, rows, lanes), BF),
            pltpu.VMEM((2, groups, rows, lanes), BF),
            pltpu.VMEM((2, groups, rows, lanes), BF),
            pltpu.VMEM((2, groups, 2 * half, lanes), BF),
            pltpu.VMEM((groups, 2 * half, lanes), BF),
            pltpu.VMEM((members, 2 * half, lanes), BF),
            pltpu.VMEM((rows, lanes), F32),
            pltpu.VMEM((members * max(half, 2 * cols) + 8 * members, lanes), F32),
            pltpu.VMEM((2, half, lanes), F32),
            pltpu.VMEM((2, half, lanes), F32),
            pltpu.VMEM((2, half, lanes), F32),
            pltpu.VMEM((2, half, lanes), F32),
            pltpu.VMEM((8, ext), F32),
            pltpu.VMEM((2, 8, ext), F32),
            pltpu.VMEM((n_bits, 2, members, lanes), F32),
            pltpu.VMEM((members, lanes), F32),
            dma((2, 3)), dma((2, 3)), dma((2, 2)), dma((2, 2)), dma((2, 1)), dma((2, 1)), dma((2,)), dma((2,)),
            dma((2,)), dma((2,)),
            dma((2, 1)), dma((2, 1)), dma((n_bits,)), dma((n_bits,)), dma((2,)),
        ],
        compiler_params=pltpu.CompilerParams(
            vmem_limit_bytes=16 * MIB, collective_id=0, has_side_effects=True),
        name="exchange",
    )(c3, e3, q, v, kf, lf, bf, packed, meta, start)

    block = next(b for b in (BLOCK, 8, 4) if members % b == 0)
    gradient, upper = pl.pallas_call(
        functools.partial(adjoint_kernel, dims, block),
        grid=(members // block,),
        in_specs=[vm] * 10,
        out_specs=[pl.BlockSpec((block, rows, lanes), lambda g: (g, 0, 0)),
                   pl.BlockSpec((members, members), lambda g: (0, 0))],
        out_shape=[sds((members, rows, lanes)), sds((members, members))],
        scratch_shapes=[pltpu.VMEM((groups, rows, lanes), F32)],
        compiler_params=pltpu.CompilerParams(vmem_limit_bytes=8 * MIB),
        name="adjoint",
    )(c3, e3, e_ext, p, px, p_edge, ka, la, ba, upper)
    return gradient.reshape(members, levels, cols, lanes), upper


def solution(mesh):
    in_specs = (
        P(None, None, "lon", "lat"),
        P(None, None, "lon", "lat"),
        P(),
        P(),
        P(),
        P("lon", "lat", None),
        P("lon", "lat"),
        P("lon", "lat", None),
        P("lon", "lat", None),
        P("lon", "lat", None),
    )
    out_specs = (P(None, None, "lon", "lat"), P())
    return jax.shard_map(shards, mesh=mesh, in_specs=in_specs, out_specs=out_specs, check_vma=False)
```

```python
import functools

import jax
import jax.numpy as jnp
from jax import lax
from jax.experimental import pallas as pl
from jax.experimental.pallas import tpu as pltpu
from jax.sharding import PartitionSpec as P

OFFSETS = (-2, -1, 1, 2)
F32, BF = jnp.float32, jnp.bfloat16
MIB = 1024 * 1024
BLOCK = 16
LARGE = 4
MESH = pl.DeviceIdType.MESH


def nn(a, b):
    return jnp.dot(a, b, preferred_element_type=F32)


def nt(a, b):
    return lax.dot_general(a, b, (((1,), (1,)), ((), ())), preferred_element_type=F32)


def tn(a, b):
    return lax.dot_general(a, b, (((0,), (0,)), ((), ())), preferred_element_type=F32)


def split(x):
    hi = x.astype(BF)
    return hi, (x - hi.astype(F32)).astype(BF)


def iota(shape, axis):
    return lax.broadcasted_iota(jnp.int32, shape, axis)


def band(diff, taps_ref, sign):
    out = jnp.where(diff == 0, 1.0, 0.0)
    for t, offset in enumerate(OFFSETS):
        out = out + jnp.where(diff == sign * offset, taps_ref[t], 0.0)
    return out


def halo_place(h, levels, cols):
    side = h // (2 * levels)
    rest = h - side * 2 * levels
    d = rest // levels
    return rest - d * levels, d + side * (cols - 2), d - 2 + side * (cols + 2)


def setup_kernel(dims, lat_hbm, lon_hbm, count_ref, e_hbm, mix_hbm, place_hbm, keep_hbm, weight_hbm, innov_hbm,
                 e_ref, kf_ref, ka_ref, lf_ref, la_ref, bf_ref, ba_ref, q_ref, v_ref, meta_ref, start_ref,
                 mix_ref, place_ref, keep_ref, weight_ref, innov_ref, lat_taps, lon_taps, sems):
    levels, cols, lanes = dims
    small = [pltpu.make_async_copy(a, b, sems.at[i]) for i, (a, b) in enumerate(
        ((mix_hbm, mix_ref), (place_hbm, place_ref), (keep_hbm, keep_ref), (weight_hbm, weight_ref),
         (innov_hbm, innov_ref), (lat_hbm, lat_taps), (lon_hbm, lon_taps)))]
    part = e_ref.shape[0] // LARGE
    large = [pltpu.make_async_copy(e_hbm.at[pl.ds(i * part, part)], e_ref.at[pl.ds(i * part, part)],
                                   sems.at[len(small) + i]) for i in range(LARGE)]
    for copy in small + large:
        copy.start()
    for copy in small:
        copy.wait()
    rows, half = levels * cols, 2 * levels
    ext = rows + 2 * half

    def ext_level_col(x):
        k, own, outer = halo_place(x - rows, levels, cols)
        inside = x < rows
        xk = x // cols
        return jnp.where(inside, xk, k), jnp.where(inside, x - xk * cols, own), jnp.where(
            inside, x - xk * cols, outer)

    diff = iota((lanes, lanes), 0) - iota((lanes, lanes), 1)
    lf_ref[...] = jnp.concatenate(split(band(diff, lat_taps, 1)), axis=0)
    la_ref[...] = jnp.concatenate(split(band(diff, lat_taps, -1)), axis=0)
    src, dst = iota((lanes, lanes), 0), iota((lanes, lanes), 1)
    member = (src // 4) == (dst // 4)
    t, u = src % 4, dst % 4
    at = jnp.where(t < 2, t - 2, lanes + t - 2) - jnp.where(u < 2, lanes - 2 + u, u - 2)
    bf_ref[...] = jnp.concatenate(split(jnp.where(member, band(at, lat_taps, 1), 0.0)), axis=0)
    ba_ref[...] = jnp.concatenate(split(jnp.where(member, band(at, lat_taps, -1), 0.0)), axis=0)
    mix = mix_ref[...]
    col = ext_level_col(iota((ext, 1), 0))[2]
    y = iota((1, rows), 1)
    taps = band((y - y // cols * cols) - col, lon_taps, 1)
    pick = (ext_level_col(iota((ext, 1), 0))[0] == iota((ext, levels), 1)).astype(F32).astype(BF)
    put = (iota((1, rows), 1) // cols == iota((levels, rows), 0)).astype(F32).astype(BF)
    kf_ref[...] = (nn(nn(pick, mix).astype(BF), put) * taps).astype(BF)
    col = ext_level_col(iota((1, ext), 1))[2]
    y = iota((rows, 1), 0)
    taps = band((y - y // cols * cols) - col, lon_taps, 1)
    pick = (ext_level_col(iota((1, ext), 1))[0] == iota((levels, ext), 0)).astype(F32).astype(BF)
    put = (iota((rows, 1), 0) // cols == iota((rows, levels), 1)).astype(F32).astype(BF)
    ka_ref[...] = (nn(put, nn(mix.T, pick).astype(BF)) * taps).astype(BF)
    slots = place_ref.shape[1]
    chunk = 512 if slots % 512 == 0 else slots
    ids_level, ids_col, _ = ext_level_col(iota((ext, 1), 0))
    ids = jnp.broadcast_to(ids_level * cols + ids_col, (ext, chunk))
    lane_ids = iota((lanes, chunk), 0)
    total = jnp.zeros((ext, 4 * lanes), F32)
    for s in range(0, slots, chunk):
        place = place_ref[:, s : s + chunk]
        r = place // lanes
        c = place - r * lanes
        live = (iota((1, chunk), 1) + s < count_ref[0, 0]).astype(F32) * keep_ref[:, s : s + chunk].astype(F32)
        q = live * weight_ref[:, s : s + chunk]
        v = q * innov_ref[:, s : s + chunk]
        hit = lane_ids == c
        parts = []
        for x in (q, v):
            for part in split(x):
                parts.append(jnp.where(hit, part.astype(F32), 0.0).astype(BF))
        total = total + nt((ids == r).astype(F32).astype(BF), jnp.concatenate(parts, axis=0))
    q = total[:, :lanes] + total[:, lanes : 2 * lanes]
    v = total[:, 2 * lanes : 3 * lanes] + total[:, 3 * lanes :]
    q_ref[...] = q[:rows]
    v_ref[...] = v[:rows]
    held = q[rows:] > 0.0
    occupied = held.astype(F32).astype(BF)
    n = 2 * half
    before = (iota((lanes, lanes), 0) < iota((lanes, lanes), 1)).astype(F32).astype(BF)
    within = nn(occupied, before)
    relative = jnp.where(held, within, -2.0 * lanes)
    count = nt(jnp.ones((8, lanes), BF), occupied).astype(BF)
    below = (iota((n, n), 0) < iota((n, n), 1)).astype(F32).astype(BF)
    start_ref[...] = nn(count, below).astype(jnp.int32)
    for side in range(2):
        at = slice(side * half, (side + 1) * half)
        meta_ref[side, 0] = relative[at]
        meta_ref[side, 1] = q[rows:][at]
        meta_ref[side, 2] = v[rows:][at]
    for copy in large:
        copy.wait()


def spot(relative_row, width):
    lanes = relative_row.shape[1]
    ranks = iota((width, lanes), 0).astype(F32)
    return jnp.where(jnp.broadcast_to(relative_row, (width, lanes)) == ranks, 1.0, 0.0).astype(BF)


def load_rows(ref, j, members, stride):
    return ref[pl.ds(j, members, stride=stride), :]


def gather_kernel(dims, start_ref, c_hbm, e_ref, meta_ref, c_ref, packed_ref, wide_a, wide_b, sum_a, sum_b, sem):
    levels, cols, lanes = dims
    members = e_ref.shape[0]
    half = 2 * levels
    per = 4
    pitch = per * cols + 8
    wide, sums = (wide_a, wide_b), (sum_a, sum_b)
    copy = pltpu.make_async_copy(c_hbm, c_ref, sem)
    copy.start()
    for ref in sums:
        ref[...] = jnp.zeros_like(ref)
    lane = iota((members, lanes), 1)

    def body(g, _):
        for k in range(2):
            base = pl.multiple_of((2 * g + k) * per * cols, per * cols)
            x = e_ref[:, pl.ds(base, per * cols), :].astype(F32)
            for m in range(members):
                wide[k][m * pitch : m * pitch + per * cols, :] = x[m]
        for k in range(2):
            found = []
            for j in range(per * cols):
                col = j % cols
                if 2 <= col < cols - 2:
                    continue
                side = int(col >= 2)
                h = (col - side * (cols - 2)) * levels + (2 * g + k) * per + j // cols
                xb = load_rows(wide[k], j, members, pitch).astype(BF)
                got = nt(xb, spot(meta_ref[side, 0, pl.ds(h, 1), :], lanes))
                first = start_ref[0, side * half + h]
                b = first // lanes
                found.append((sums[side], b, first - b * lanes, got))
            for ref, b, shift, got in found:
                got = pltpu.roll(got, shift, 1)
                ref[b] += jnp.where(lane >= shift, got, 0.0)
                ref[b + 1] += jnp.where(lane < shift, got, 0.0)
        return 0

    lax.fori_loop(0, levels // (2 * per), body, 0)
    for b in range(packed_ref.shape[0]):
        packed_ref[b] = (sum_a[b] + sum_b[b]).astype(BF)
    copy.wait()


def factor(s_ref, out_ref, size):
    lanes = s_ref.shape[1]
    step = 8
    lane = iota((step, lanes), 1)
    row = iota((step, lanes), 0)
    for b in range(0, size, step):
        panel = s_ref[b : b + step, :]
        cols = [jnp.broadcast_to(panel[:, b + i : b + i + 1], (step, lanes)) for i in range(step)]
        done = jnp.zeros((step, lanes), F32)
        for j in range(step):
            scale = lax.rsqrt(jnp.broadcast_to(cols[j][j : j + 1], (step, lanes)))
            across = jnp.broadcast_to(panel[j : j + 1], (step, lanes)) * scale
            done = jnp.where(row == j, across, done)
            down = cols[j] * scale
            panel = panel - down * across
            for i in range(j + 1, step):
                cols[i] = cols[i] - down * jnp.broadcast_to(down[i : i + 1], (step, lanes))
        done = jnp.where(lane >= b + row, done, 0.0)
        out_ref[b : b + step, :] = done[:, :size]
        if b + step < size:
            hi, lo = split(done)
            low = jnp.concatenate([hi, hi, lo], axis=0)
            high = jnp.concatenate([hi, lo, hi], axis=0)
            s_ref[...] = s_ref[...] - tn(low, high)[:size]


def forward_loop(group, c_ref, e_ref, kf_ref, lf_ref, inc_ref, outer_ref, first, last):
    rows, lanes = inc_ref.shape
    ext = rows + outer_ref.shape[1]

    def body(step, _):
        for quad in range(0, group, 4):
            at = [group * step + quad + i for i in range(4)]
            smooth = []
            for m in at:
                x = c_ref[m]
                smooth.append(nn(jnp.concatenate([x, x], axis=1), lf_ref[...]).astype(BF))
            out = [nn(kf_ref[...], jnp.concatenate(smooth[2 * i : 2 * i + 2], axis=1)) for i in range(2)]
            total = inc_ref[...]
            for i, m in enumerate(at):
                part = out[i // 2][:, i % 2 * lanes : (i % 2 + 1) * lanes]
                total = total + e_ref[m].astype(F32) * part[:rows]
                outer_ref[m] = part[rows:].astype(BF)
            inc_ref[...] = total
        return 0

    lax.fori_loop(first, last, body, 0)


def exchange_kernel(dims, sizes, c_ref, e_ref, q_ref, v_ref, kf_ref, lf_ref, bf_ref, packed_ref, meta_ref,
                    start_ref,
                    p_ref, px_ref, ext_ref, edge_ref, upper_ref,
                    got_left, got_right, got_meta, got_start, start_smem, own_c, own_e, lat_c, lat_e, lat_x, own_x, outer_ref,
                    inc_ref, wide_ref, send_part, got_part, send_give, got_give, p_edge, got_edge, gram_in, total_ref,
                    far_sem, far_recv, lat_sem, lat_recv, x_sem, x_recv, inc_sem, inc_recv, give_sem, give_recv,
                    pe_sem, pe_recv, gram_sem, gram_recv, smem_sem):
    levels, cols, lanes = dims
    n_lat, n_lon = sizes
    members, rows = c_ref.shape[0], c_ref.shape[1]
    half = 2 * levels
    ext = rows + 2 * half
    per = lanes // 4
    groups = own_e.shape[0]
    lat, lon = lax.axis_index("lat"), lax.axis_index("lon")
    left, right = lax.rem(lon + n_lon - 1, n_lon), lax.rem(lon + 1, n_lon)
    has_before, has_after = lat > 0, lat < n_lat - 1

    def flip(x, bit):
        return x + bit - 2 * bit * (x // bit - x // (2 * bit) * 2)

    partners = [("lat", 1 << i) for i in range(n_lat.bit_length() - 1)]
    n_near = len(partners)
    partners += [("lon", 1 << i) for i in range(n_lon.bit_length() - 1)]
    barrier = pltpu.get_barrier_semaphore()

    def greet(where):
        pl.semaphore_signal(barrier, inc=1, device_id=where, device_id_type=MESH)

    greet({"lon": left})
    greet({"lon": right})

    @pl.when(has_before)
    def _():
        greet({"lat": lat - 1})

    @pl.when(has_after)
    def _():
        greet({"lat": lat + 1})

    for axis, bit in partners:
        greet({axis: flip(lat if axis == "lat" else lon, bit)})

    packed_at = iota((rows, lanes), 1) // 4

    def pack_edges(ref, own):
        for g in range(groups):
            first, last = g * per, min((g + 1) * per, members)

            def pack(k, x, first=first):
                for i in range(4):
                    m = first + 4 * k + i
                    x = jnp.where(packed_at == m - first, pltpu.roll(ref[m], 2 + 4 * (m - first), 1), x)
                return x

            own[g] = lax.fori_loop(0, (last - first) // 4, pack, jnp.zeros((rows, lanes), BF))

    pack_edges(c_ref, own_c)
    pl.semaphore_wait(barrier, 2 + len(partners) + has_before.astype(jnp.int32) + has_after.astype(jnp.int32))

    def remote(src, dst, s, r, where):
        return pltpu.make_async_remote_copy(
            src_ref=src, dst_ref=dst, send_sem=s, recv_sem=r, device_id=where, device_id_type=MESH)

    blocks = packed_ref.shape[0]
    got = (got_left, got_right)
    far = []
    for slot, to in ((0, right), (1, left)):
        mine = 1 - slot
        far.append([
            remote(meta_ref.at[mine], got_meta.at[slot], far_sem.at[slot, 0], far_recv.at[slot, 0], {"lon": to}),
            remote(start_ref, got_start.at[slot], far_sem.at[slot, 1], far_recv.at[slot, 1], {"lon": to}),
            remote(packed_ref, got[slot].at[pl.ds(0, blocks)], far_sem.at[slot, 2], far_recv.at[slot, 2],
                   {"lon": to})])

    def lat_pair(src, dst, s, r, k):
        up = remote(src, dst.at[0], s.at[0, k], r.at[0, k], {"lat": lat + 1})
        down = remote(src, dst.at[1], s.at[1, k], r.at[1, k], {"lat": lat - 1})
        return up, down

    def lat_start(up, down):
        pl.when(has_after)(up.start)
        pl.when(has_before)(down.start)

    def lat_wait(up, down):
        pl.when(has_after)(up.wait_send)
        pl.when(has_before)(down.wait_send)
        pl.when(has_before)(up.wait_recv)
        pl.when(has_after)(down.wait_recv)

    for copies in far:
        for copy in copies[:2]:
            copy.start()
    wraps_left = lon == 0

    @pl.when(wraps_left)
    def _():
        far[1][2].start()
        far[0][2].start()

    @pl.when(jnp.logical_not(wraps_left))
    def _():
        far[0][2].start()
        far[1][2].start()

    near = lat_pair(own_c, lat_c, lat_sem, lat_recv, 0)
    lat_start(*near)

    for side, missing in ((0, jnp.logical_not(has_before)), (1, jnp.logical_not(has_after))):
        @pl.when(missing)
        def _(side=side):
            for ref in (lat_c, lat_e, lat_x, got_edge):
                ref[side] = jnp.zeros_like(ref[side])

    for slot in range(2):
        got[slot][blocks:] = jnp.zeros_like(got[slot][blocks:])
    inc_ref[...] = jnp.zeros_like(inc_ref)

    two = 2
    pitch = two * cols + 8

    def grams(g, gram):
        gram = list(gram)
        base = pl.multiple_of(g * two * cols, two * cols)
        x = e_ref[:, pl.ds(base, two * cols), :].astype(F32)
        for m in range(members):
            wide_ref[m * pitch : m * pitch + two * cols, :] = x[m]
        weight = q_ref[pl.ds(base, two * cols), :]
        for pair in range(0, two * cols, 2):
            plain, his, los = [], [], []
            for j in (pair, pair + 1):
                y = load_rows(wide_ref, j, members, pitch)
                plain.append(y.astype(BF))
                hi, lo = split(y * weight[j : j + 1])
                his.append(hi)
                los.append(lo)
            weighted = jnp.concatenate([jnp.concatenate(his, axis=1), jnp.concatenate(los, axis=1)], axis=0)
            k = pair // 2 % 2
            gram[k] = gram[k] + nt(weighted, jnp.concatenate(plain, axis=1))
        return tuple(gram)

    zero = jnp.zeros((2 * members, members), F32)
    gram = lax.fori_loop(0, levels // two, grams, (zero, zero))
    gram = gram[0] + gram[1]
    total_ref[...] = jnp.zeros_like(total_ref)
    total_ref[:, :members] = gram[:members] + gram[members:]

    stages, ended = [], []

    def stage_start():
        i = len(stages)
        if i < len(partners):
            axis, bit = partners[i]
            gram_in[i, 0] = total_ref[...]
            copy = remote(gram_in.at[i, 0], gram_in.at[i, 1], gram_sem.at[i], gram_recv.at[i],
                          {axis: flip(lat if axis == "lat" else lon, bit)})
            copy.start()
            stages.append(copy)

    def stage_end():
        if len(ended) < len(stages):
            i = len(ended)
            stages[i].wait()
            total_ref[...] = total_ref[...] + gram_in[i, 1]
            ended.append(i)

    group = 8 if members % 8 == 0 else 4
    span = 16 if members % 16 == 0 else group
    turns = members // span
    cuts = [0, 0] + [min(i, turns) for i in range(1, n_near)] + [turns] if n_near else [0, turns]
    for i in range(n_near + 1):
        stage_start()
        if i == 0:
            pack_edges(e_ref, own_e)
        forward_loop(span, c_ref, e_ref, kf_ref, lf_ref, inc_ref, outer_ref, cuts[i], cuts[i + 1])
        if i < n_near:
            stage_end()

    lat_wait(*near)
    near_e = lat_pair(own_e, lat_e, lat_sem, lat_recv, 1)
    lat_start(*near_e)
    before = iota((rows, lanes), 1) % 4 < 2
    spare = []
    for g in range(groups):
        halo = jnp.where(before, lat_c[0, g].astype(F32), lat_c[1, g].astype(F32)).astype(BF)
        mixed = nn(kf_ref[...], halo).astype(BF)
        spare.append(nn(jnp.concatenate([mixed, mixed], axis=1), bf_ref[...]))
    source = iota((lanes, lanes), 0) % 4
    target = iota((lanes, lanes), 1)
    drop = (target == jnp.where(source < 2, lanes - 2 + source, source - 2)).astype(F32).astype(BF)

    def settle(products):
        total = None
        for x in products:
            part = nn(jnp.concatenate(split(x), axis=1), jnp.concatenate([drop, drop], axis=0))
            total = part if total is None else total + part
        return total

    inc_ref[...] += settle([own_e[g].astype(F32) * spare[g][:rows] for g in range(groups)])

    for d in range(2):
        at = slice(d * levels, (d + 1) * levels)
        send_part[0, at] = inc_ref[pl.ds(cols - 2 + d, levels, stride=cols), :]
        send_part[1, at] = inc_ref[pl.ds(d, levels, stride=cols), :]
    swap = []
    for slot, to in ((0, right), (1, left)):
        swap.append(remote(send_part.at[slot], got_part.at[slot], inc_sem.at[slot], inc_recv.at[slot], {"lon": to}))
        swap[-1].start()

    local = []
    for slot in range(2):
        for copy in far[slot][:2]:
            copy.wait()
        local.append(pltpu.make_async_copy(got_start.at[slot], start_smem.at[slot], smem_sem.at[slot]))
        local[-1].start()
    for copy in local:
        copy.wait()
    pitch_x = half + 8
    for slot in range(2):
        far[slot][2].wait()

        def expand(k, _, slot=slot):
            for i in range(8):
                h = k * 8 + i
                start = start_smem[slot, 0, (1 - slot) * half + h]
                b = start // lanes
                shift = (start - b * lanes).astype(F32)
                hot = spot(got_meta[slot, 0, pl.ds(h, 1), :] + shift, 2 * lanes)
                x = nn(jnp.concatenate([got[slot][b], got[slot][b + 1]], axis=1), hot)
                wide_ref[pl.ds(h, members, stride=pitch_x), :] = x
            return 0

        lax.fori_loop(0, half // 8, expand, 0)
        if len(stages) > n_near:
            stage_end()
            stage_start()
        at_x = slice(slot * half, (slot + 1) * half)
        given = jnp.zeros((half, lanes), F32)
        for g in range(groups):
            first, last = g * per, min((g + 1) * per, members)

            def outer(k, carry, first=first, at_x=at_x):
                total, edges = carry
                for i in range(group):
                    m = first + group * k + i
                    x = wide_ref[pl.ds(pl.multiple_of(m * pitch_x, 8), half), :]
                    xb = x.astype(BF)
                    ext_ref[m, at_x] = xb
                    total = total + x * outer_ref[m, at_x].astype(F32)
                    edges = jnp.where(packed_at[:half] == m - first, pltpu.roll(xb, 2 + 4 * (m - first), 1), edges)
                return total, edges

            given, edges = lax.fori_loop(0, (last - first) // group, outer, (given, jnp.zeros((half, lanes), BF)))
            own_x[g, at_x] = edges
        from_row = rows + slot * half
        send_give[slot] = given + settle(
            [own_x[g, at_x].astype(F32) * spare[g][from_row : from_row + half] for g in range(groups)])
        swap.append(remote(send_give.at[slot], got_give.at[1 - slot], give_sem.at[slot], give_recv.at[1 - slot],
                           {"lon": (left, right)[slot]}))
        swap[-1].start()
    across = lat_pair(own_x, lat_x, x_sem, x_recv, 0)
    lat_start(*across)

    while len(ended) < len(partners):
        stage_end()
        stage_start()
    eye = (iota((members, lanes), 0) == iota((members, lanes), 1)).astype(F32)
    total_obs = packed_ref.shape[0] * lanes * n_lat * n_lon
    total_ref[...] = eye + members / total_obs * total_ref[...]
    factor(total_ref, upper_ref, members)

    for copy in swap:
        copy.wait()
    for slot in range(2):
        px_ref[slot * half : (slot + 1) * half] = (
            got_meta[slot, 1] * (got_part[slot] + send_give[slot]) - got_meta[slot, 2])
        for d in range(2):
            at = pl.ds(slot * (cols - 2) + d, levels, stride=cols)
            inc_ref[at, :] = inc_ref[at, :] + got_give[slot, d * levels : (d + 1) * levels]
    p_ref[...] = q_ref[...] * inc_ref[...] - v_ref[...]

    edge_row, edge_lane = iota((8, lanes), 0), iota((8, lanes), 1)
    pick = jnp.where(edge_lane == jnp.where(edge_row < 2, lanes - 2 + edge_row, edge_row - 2), 1.0, 0.0)
    pick = jnp.where(edge_row < 4, pick, 0.0).astype(BF)
    for ref, at in ((p_ref, slice(0, rows)), (px_ref, slice(rows, ext))):
        hi, lo = split(ref[...])
        p_edge[:, at] = nt(pick, hi) + nt(pick, lo)
    lat_wait(*near_e)
    final = lat_pair(p_edge, got_edge, pe_sem, pe_recv, 0)
    lat_start(*final)
    lat_wait(*across)
    before = iota((ext, lanes), 1) % 4 < 2
    halo = []
    for g in range(groups):
        far_e = [jnp.concatenate([lat_e[side, g], lat_x[side, g]], axis=0).astype(F32) for side in range(2)]
        halo.append(jnp.where(before, far_e[0], far_e[1]))
    spread = jnp.where((edge_lane % 4 == edge_row) & (edge_row < 4), 1.0, 0.0).astype(BF)
    lat_wait(*final)
    p_halo = jnp.where(iota((8, ext), 0) < 2, got_edge[0], got_edge[1])
    hi, lo = split(p_halo)
    p_halo = tn(hi, spread) + tn(lo, spread)
    for g in range(groups):
        edge_ref[g] = (halo[g] * p_halo).astype(BF)


def adjoint_kernel(dims, block, c_ref, e_ref, ext_ref, p_ref, px_ref, pe_ref, ka_ref, la_ref, ba_ref, upper_ref,
                   out_ref, upper_out, edge_ref):
    levels, cols, lanes = dims
    members, rows = c_ref.shape[0], c_ref.shape[1]
    step = pl.program_id(0)
    per = lanes // 4

    @pl.when(step == 0)
    def _():
        upper_out[...] = upper_ref[...]
        for g in range(edge_ref.shape[0]):
            z = nn(ka_ref[...], pe_ref[g]).astype(BF)
            edge_ref[g] = nn(jnp.concatenate([z, z], axis=1), ba_ref[...])

    lane = iota((rows, lanes), 1)
    at_edge = (lane < 2) | (lane >= lanes - 2)
    p, px = p_ref[...], px_ref[...]

    for quad in range(block // 4):
        wide = []
        for i in range(4):
            m = step * block + 4 * quad + i
            own = (e_ref[m].astype(F32) * p).astype(BF)
            far = (ext_ref[m].astype(F32) * px).astype(BF)
            wide.append(jnp.concatenate([own, far], axis=0))
        mixed = [nn(ka_ref[...], jnp.concatenate(wide[2 * i : 2 * i + 2], axis=1)).astype(BF) for i in range(2)]
        smooth = []
        for i in range(4):
            z = mixed[i // 2][:, i % 2 * lanes : (i % 2 + 1) * lanes]
            smooth.append(nn(jnp.concatenate([z, z], axis=1), la_ref[...]))
        for i in range(4):
            m = step * block + 4 * quad + i
            g = m // per
            turned = pltpu.roll(edge_ref[g], lax.rem(2 * lanes - 2 - 4 * (m - g * per), lanes), 1)
            out_ref[4 * quad + i] = c_ref[m].astype(F32) + smooth[i] + jnp.where(at_edge, turned, 0.0)


def shards(
    control, ensemble, level_mix, lat_taps, lon_taps, obs_location, obs_count, obs_keep, innovation, obs_weight
):
    members, levels, cols, lanes = control.shape
    dims = (levels, cols, lanes)
    rows, half = levels * cols, 2 * levels
    ext = rows + 2 * half
    slots = obs_location.shape[2]
    blocks = slots // lanes
    groups = -(-4 * members // lanes)
    n_lat, n_lon = lax.axis_size("lat"), lax.axis_size("lon")
    vm, sm = pl.BlockSpec(memory_space=pltpu.VMEM), pl.BlockSpec(memory_space=pltpu.SMEM)
    hbm = pl.BlockSpec(memory_space=pltpu.HBM)
    dma = pltpu.SemaphoreType.DMA
    away = functools.partial(pltpu.with_memory_space_constraint, memory_space=pltpu.HBM)

    def sds(shape, dtype=F32):
        return jax.ShapeDtypeStruct(shape, dtype)

    e3, kf, ka, lf, la, bf, ba, q, v, meta, start = pl.pallas_call(
        functools.partial(setup_kernel, dims),
        in_specs=[hbm, hbm, sm] + [hbm] * 6,
        out_specs=[vm] * 11,
        out_shape=[sds((members, rows, lanes), BF), sds((ext, rows), BF), sds((rows, ext), BF)]
        + [sds((2 * lanes, lanes), BF)] * 4
        + [sds((rows, lanes)), sds((rows, lanes)), sds((2, 3, half, lanes)), sds((8, 2 * half), jnp.int32)],
        scratch_shapes=[pltpu.VMEM((levels, levels), BF), pltpu.VMEM((1, slots), jnp.int32),
                        pltpu.VMEM((1, slots), jnp.int32), pltpu.VMEM((1, slots), F32), pltpu.VMEM((1, slots), F32),
                        pltpu.SMEM((4,), F32), pltpu.SMEM((4,), F32), dma((7 + LARGE,))],
        compiler_params=pltpu.CompilerParams(vmem_limit_bytes=8 * MIB),
        name="setup",
    )(away(lat_taps), away(lon_taps), obs_count, away(ensemble.reshape(members, rows, lanes)), away(level_mix),
      away(obs_location[0]), away(obs_keep[0]), away(obs_weight[0]), away(innovation[0]))

    c3, packed = pl.pallas_call(
        functools.partial(gather_kernel, dims),
        in_specs=[sm, hbm, vm, vm],
        out_specs=[vm] * 2,
        out_shape=[sds((members, rows, lanes), BF), sds((blocks, members, lanes), BF)],
        scratch_shapes=[*[pltpu.VMEM((members * (4 * cols + 8), lanes), F32)] * 2,
                        *[pltpu.VMEM((blocks + 2, members, lanes), F32)] * 2, dma],
        compiler_params=pltpu.CompilerParams(vmem_limit_bytes=8 * MIB),
        name="gather",
    )(start, away(control.reshape(members, rows, lanes)), e3, meta)

    n_bits = (n_lat.bit_length() - 1) + (n_lon.bit_length() - 1)
    p, px, e_ext, p_edge, upper = pl.pallas_call(
        functools.partial(exchange_kernel, dims, (n_lat, n_lon)),
        in_specs=[vm] * 10,
        out_specs=[vm] * 5,
        out_shape=[sds((rows, lanes)), sds((2 * half, lanes)), sds((members, 2 * half, lanes), BF),
                   sds((groups, ext, lanes), BF), sds((members, members))],
        scratch_shapes=[
            pltpu.VMEM((blocks + 2, members, lanes), BF),
            pltpu.VMEM((blocks + 2, members, lanes), BF),
            pltpu.VMEM((2, 3, half, lanes), F32),
            pltpu.VMEM((2, 8, 2 * half), jnp.int32),
            pltpu.SMEM((2, 8, 2 * half), jnp.int32),
            pltpu.VMEM((groups, rows, lanes), BF),
            pltpu.VMEM((groups, rows, lanes), BF),
            pltpu.VMEM((2, groups, rows, lanes), BF),
            pltpu.VMEM((2, groups, rows, lanes), BF),
            pltpu.VMEM((2, groups, 2 * half, lanes), BF),
            pltpu.VMEM((groups, 2 * half, lanes), BF),
            pltpu.VMEM((members, 2 * half, lanes), BF),
            pltpu.VMEM((rows, lanes), F32),
            pltpu.VMEM((members * max(half, 2 * cols) + 8 * members, lanes), F32),
            pltpu.VMEM((2, half, lanes), F32),
            pltpu.VMEM((2, half, lanes), F32),
            pltpu.VMEM((2, half, lanes), F32),
            pltpu.VMEM((2, half, lanes), F32),
            pltpu.VMEM((8, ext), F32),
            pltpu.VMEM((2, 8, ext), F32),
            pltpu.VMEM((n_bits, 2, members, lanes), F32),
            pltpu.VMEM((members, lanes), F32),
            dma((2, 3)), dma((2, 3)), dma((2, 2)), dma((2, 2)), dma((2, 1)), dma((2, 1)), dma((2,)), dma((2,)),
            dma((2,)), dma((2,)),
            dma((2, 1)), dma((2, 1)), dma((n_bits,)), dma((n_bits,)), dma((2,)),
        ],
        compiler_params=pltpu.CompilerParams(
            vmem_limit_bytes=16 * MIB, collective_id=0, has_side_effects=True),
        name="exchange",
    )(c3, e3, q, v, kf, lf, bf, packed, meta, start)

    block = next(b for b in (BLOCK, 8, 4) if members % b == 0)
    gradient, upper = pl.pallas_call(
        functools.partial(adjoint_kernel, dims, block),
        grid=(members // block,),
        in_specs=[vm] * 10,
        out_specs=[pl.BlockSpec((block, rows, lanes), lambda g: (g, 0, 0)),
                   pl.BlockSpec((members, members), lambda g: (0, 0))],
        out_shape=[sds((members, rows, lanes)), sds((members, members))],
        scratch_shapes=[pltpu.VMEM((groups, rows, lanes), F32)],
        compiler_params=pltpu.CompilerParams(vmem_limit_bytes=8 * MIB),
        name="adjoint",
    )(c3, e3, e_ext, p, px, p_edge, ka, la, ba, upper)
    return gradient.reshape(members, levels, cols, lanes), upper


def solution(mesh):
    in_specs = (
        P(None, None, "lon", "lat"),
        P(None, None, "lon", "lat"),
        P(),
        P(),
        P(),
        P("lon", "lat", None),
        P("lon", "lat"),
        P("lon", "lat", None),
        P("lon", "lat", None),
        P("lon", "lat", None),
    )
    out_specs = (P(None, None, "lon", "lat"), P())
    return jax.shard_map(shards, mesh=mesh, in_specs=in_specs, out_specs=out_specs, check_vma=False)
```
